32 devices in a mesh: lon: 8 (over y, x, core), lev: 4 (over z).
Axes of the slice: x: 2, y: 2, z: 4, core: 2. Of those that a mesh axis runs over, the one named last changes fastest.
Arguments:
- tracers: float32 [32, 16, 64, 1024], P(None, 'lev', None, 'lon'), may hold values from 0.1 to 10
- offsets: int32 [64], replicated, may hold values from 0 to 1023
- fraction: float32 [64], replicated, may hold values from 0 to 1
- bin_class: int32 [8], replicated, may hold values from 0 to 7
- thickness: float32 [16], P('lev'), may hold values from 0.5 to 2
Outputs:
- settled: float32 [32, 16, 64, 1024], P(None, 'lev', None, 'lon')
The draws below stay inside these ranges and needn't reach their ends.
All inputs are finite; a program needn't handle non-finite values.
Results may differ from the reference program's by a relative error of at most 0.00002.
Values sent between devices are 32-bit elements; how exact they have to be, the bound alone decides.
A program may use at most 128 MiB of HBM per device.

```python
import math
import jax
import jax.numpy as jnp
from jax import lax

GROUPS = 4
TRACERS = 32
NCLASS = 8
NLAT = 64
WBINS = 8
NLON = 1024
NLEV = 16


def touch_ends(array, key, smallest, high):
    index_at = [jax.random.randint(jax.random.fold_in(key, axis), (), 0, length) for axis, length in enumerate(array.shape)]
    longest = array.shape.index(max(array.shape))
    next_to = index_at[:longest] + [(index_at[longest] + 1) % array.shape[longest]] + index_at[longest + 1:]
    return array.at[tuple(index_at)].set(smallest).at[tuple(next_to)].set(high)


def block_scale(stream_key, dims, shards, low, largest):
    gain, own = 1.0, jax.random.fold_in(stream_key, 6)
    for position, shards_of in shards:
        heights = jnp.exp(jax.random.uniform(jax.random.fold_in(own, position), (shards_of,), jnp.float32, low / len(shards), largest / len(shards)))
        gain = gain * jnp.repeat(heights, dims[position] // shards_of).reshape([-1 if axis == position else 1 for axis in range(len(dims))])
    return gain


def setup_inputs(seed: int = 0) -> dict:
    splits = jax.random.split(jax.random.key(seed), 6)
    return {
        "tracers": jnp.clip(jnp.exp(math.log(10.0) - 4.6051702 * jax.random.uniform(splits[0], (TRACERS, NLEV, NLAT, NLON), jnp.float32) ** block_scale(splits[0], (TRACERS, NLEV, NLAT, NLON), ((1, 4), (3, 8)), -0.2, 0.2)), 0.1, 10.0),
        "offsets": touch_ends(jax.random.randint(splits[1], (NLAT,), 0, NLON), jax.random.fold_in(splits[1], 1), 0, NLON - 1).astype(jnp.int32),
        "fraction": jnp.clip(jax.random.uniform(splits[2], (NLAT,), jnp.float32, 0.0, 1.0), 0.0, 1.0),
        "bin_class": touch_ends(jax.random.randint(splits[3], (WBINS,), 0, NCLASS), jax.random.fold_in(splits[3], 1), 0, NCLASS - 1).astype(jnp.int32),
        "thickness": jnp.clip(jnp.exp(math.log(2.0) - 1.3862944 * jax.random.uniform(splits[4], (NLEV,), jnp.float32) ** block_scale(splits[4], (NLEV,), ((0, 4),), -0.2, 0.2)), 0.5, 2.0),
    }


def reference(tracers, offsets, fraction, bin_class, thickness):
    nlon = tracers.shape[-1]
    nlat = tracers.shape[2]
    cells = jnp.arange(nlon, dtype=jnp.int32)
    first = (cells[None, :] - offsets[:, None]) % nlon
    second = (first - 1) % nlon
    rows = jnp.arange(nlat, dtype=jnp.int32)[:, None]
    share = fraction[:, None]

    def move(field):
        return (1.0 - share) * field[:, rows, first] + share * field[:, rows, second]

    moved = lax.map(move, tracers)
    speed = 0.5 * jnp.exp2(jnp.repeat(bin_class, GROUPS).astype(jnp.float32))
    ratio = speed[:, None] / thickness[None, :]

    def level(carry, inputs):
        column, rate = inputs
        rate = rate[:, None, None]
        value = (column + rate * carry) / (1.0 + rate)
        return value, value

    start = jnp.zeros((tracers.shape[0], nlat, nlon), jnp.float32)
    _, settled = lax.scan(level, start, (jnp.swapaxes(moved, 0, 1), ratio.T))
    return jnp.swapaxes(settled, 0, 1)
```

```python
import functools

import jax
import jax.numpy as jnp
from jax import lax
from jax.experimental import pallas as pl
from jax.experimental.pallas import tpu as pltpu
from jax.sharding import PartitionSpec as P

GROUPS = 4
SUB = 8
PIECES = 8
HOLD = 3
SHARES = (36, 40, 44, 48, 56)


def exchange_kernel(
    n, depth, x_ref, offsets_hbm, fraction_hbm, class_hbm, thick_hbm, out_ref,
    offsets_ref, fraction_ref, class_ref, thick_ref, small, recv, obuf, zin, row_ref, share_ref, s1, r1, s2, r2, own1, own2, zs, zr,
):
    tracers, levels, lats, width = x_ref.shape
    mine = tracers // n
    halves = max(1, min(PIECES // mine, lats // SUB))
    rows_of = lats // halves
    me = lax.axis_index("lon")
    lev = lax.axis_index("lev")

    def at(c):
        return c // halves, pl.ds(pl.multiple_of((c % halves) * rows_of, SUB), rows_of)

    def peer(k):
        return lax.rem(me + k, n)

    def outward(tt, k):
        return pltpu.make_async_remote_copy(
            src_ref=x_ref.at[peer(k) * mine + tt],
            dst_ref=recv.at[me, tt],
            send_sem=s1.at[tt, k], recv_sem=r1.at[tt, k],
            device_id={"lon": peer(k)}, device_id_type=pl.DeviceIdType.MESH,
        )

    def homeward(tt, k):
        return pltpu.make_async_remote_copy(
            src_ref=obuf.at[peer(k), tt],
            dst_ref=out_ref.at[me * mine + tt],
            send_sem=s2.at[tt, k], recv_sem=r2.at[tt, k],
            device_id={"lon": peer(k)}, device_id_type=pl.DeviceIdType.MESH,
        )

    def downward(c):
        tt, rows = at(c)
        return pltpu.make_async_remote_copy(
            src_ref=obuf.at[:, tt, levels - 1, rows, :],
            dst_ref=zin.at[:, tt, rows, :],
            send_sem=zs.at[c], recv_sem=zr.at[c],
            device_id={"lev": lax.rem(lev + 1, depth)}, device_id_type=pl.DeviceIdType.MESH,
        )

    def own_in(tt):
        return pltpu.make_async_copy(x_ref.at[me * mine + tt], recv.at[me, tt], own1.at[tt])

    def own_out(tt):
        return pltpu.make_async_copy(obuf.at[me, tt], out_ref.at[me * mine + tt], own2.at[tt])

    scalars = [
        pltpu.make_async_copy(source, held, small.at[i])
        for i, (source, held) in enumerate((
            (offsets_hbm, offsets_ref), (fraction_hbm, fraction_ref),
            (class_hbm, class_ref), (thick_hbm, thick_ref)))
    ]
    for copy in scalars:
        copy.start()

    barrier = pltpu.get_barrier_semaphore()
    for k in range(1, n):
        pl.semaphore_signal(barrier, inc=1, device_id={"lon": peer(k)},
                            device_id_type=pl.DeviceIdType.MESH)
    for k in (1, depth - 1):
        pl.semaphore_signal(barrier, inc=1, device_id={"lev": lax.rem(lev + k, depth)},
                            device_id_type=pl.DeviceIdType.MESH)
    pl.semaphore_wait(barrier, n + 1)

    count = mine * halves

    @pl.loop(0, mine)
    def _(tt):
        @pl.loop(1, n)
        def _(k):
            outward(tt, k).start()

        own_in(tt).start()

    for copy in scalars:
        copy.wait()

    @pl.loop(0, lats)
    def _(j):
        shift = jnp.full((1, width), offsets_ref[j], jnp.int32)
        row_ref[pl.ds(j, 1), :] = shift
        share_ref[pl.ds(j, 1), :] = jnp.full((1, width), fraction_ref[j], jnp.float32)

    def ratios(tracer):
        bin_class = jnp.full((SUB, width), class_ref[tracer // GROUPS], jnp.int32)
        speed = 0.5
        for b in range(3):
            speed = speed * jnp.where((bin_class & (1 << b)) != 0, 2.0 ** (1 << b), 1.0)
        return [speed / thick_ref[level] for level in range(levels)]

    lane = lax.broadcasted_iota(jnp.int32, (SUB, width), 1)

    def behind(value, by):
        by %= n
        if by == 0:
            return value
        return jnp.concatenate([value[n - by:], value[:n - by]], axis=0)

    def turn(c):
        tt = c // halves
        base = (c % halves) * rows_of
        ratio = ratios(me * mine + tt)
        keep = [1.0 / (1.0 + r) for r in ratio]
        carry = [r * k for r, k in zip(ratio, keep)]

        @pl.when(c % halves == 0)
        def _():
            own_in(tt).wait()

            @pl.loop(1, n)
            def _(k):
                outward(tt, k).wait_recv()

        @pl.loop(0, rows_of // SUB)
        def _(g):
            rows = pl.ds(pl.multiple_of(base + g * SUB, SUB), SUB)
            shift = row_ref[rows, :]
            remainder = lax.rem(shift, width)
            quotient = lax.div(shift, width)
            share = share_ref[rows, :]
            fine = [(remainder & (1 << b)) != 0 for b in range((width - 1).bit_length())]
            coarse = [(quotient & (1 << b)) != 0 for b in range((n - 1).bit_length())]
            same_block = lane >= remainder
            first_lane = lane == 0
            value = None
            for level in range(levels):
                field = recv[:, tt, level, rows, :]
                turned = pltpu.roll(field, 1, axis=2)
                left = jnp.where(first_lane[None], behind(turned, 1), turned)
                field = (1.0 - share)[None] * field + share[None] * left
                for b, chosen in enumerate(fine):
                    field = jnp.where(chosen[None], pltpu.roll(field, 1 << b, axis=2), field)
                field = jnp.where(same_block[None], field, behind(field, 1))
                for b, chosen in enumerate(coarse):
                    field = jnp.where(chosen[None], behind(field, 1 << b), field)
                field = keep[level][None] * field
                value = field if value is None else field + carry[level][None] * value
                obuf[:, tt, level, rows, :] = value

    def settle(c):
        tt = c // halves
        base = (c % halves) * rows_of
        reach = []
        for r in ratios(me * mine + tt):
            step = r / (1.0 + r)
            reach.append(reach[-1] * step if reach else step)

        def add_above(level):
            @pl.loop(0, rows_of // SUB)
            def _(g):
                rows = pl.ds(pl.multiple_of(base + g * SUB, SUB), SUB)
                obuf[:, tt, level, rows, :] += reach[level][None] * zin[:, tt, rows, :]

        @pl.when(lev > 0)
        def _():
            downward(c).wait_recv()
            add_above(levels - 1)

        @pl.when(lev < depth - 1)
        def _():
            downward(c).start()

        @pl.when(lev > 0)
        def _():
            for level in range(levels - 1):
                add_above(level)

    def send_home(tt):
        @pl.loop(1, n)
        def _(k):
            homeward(tt, k).start()

        own_out(tt).start()

    hold = min(HOLD, count - 1)

    @pl.loop(0, count + depth - 1)
    def _(i):
        @pl.when(i < count)
        def _():
            turn(i)

        done = i - lev

        @pl.when((done >= 0) & (done < count))
        def _():
            settle(done)

        @pl.when((done >= 0) & (done < count) & (done % halves == halves - 1) & (i > hold))
        def _():
            send_home(done // halves)

        @pl.when(i == hold)
        def _():
            @pl.loop(0, mine)
            def _(tt):
                @pl.when((tt + 1) * halves - 1 <= done)
                def _():
                    send_home(tt)

    @pl.when(lev < depth - 1)
    def _():
        @pl.loop(0, count)
        def _(c):
            downward(c).wait_send()

    @pl.loop(0, mine)
    def _(tt):
        own_out(tt).wait()

        @pl.loop(1, n)
        def _(k):
            outward(tt, k).wait_send()
            homeward(tt, k).wait()


def by_tracer(tracers, offsets, fraction, bin_class, thickness):
    count, levels, lats, width = tracers.shape
    n = lax.axis_size("lon")
    depth = lax.axis_size("lev")
    mine = count // n
    pieces = mine * max(1, min(PIECES // mine, lats // SUB))
    hbm = pl.BlockSpec(memory_space=pltpu.HBM)
    held = [pltpu.SMEM(a.shape, a.dtype) for a in (offsets, fraction, bin_class, thickness)]
    sem = pltpu.SemaphoreType.DMA
    return pl.pallas_call(
        functools.partial(exchange_kernel, n, depth),
        out_shape=jax.ShapeDtypeStruct(tracers.shape, jnp.float32),
        in_specs=[hbm] * 5,
        out_specs=pl.BlockSpec(memory_space=pl.ANY),
        scratch_shapes=[
            *held, sem((4,)),
            pltpu.VMEM((n, mine, levels, lats, width), jnp.float32),
            pltpu.VMEM((n, mine, levels, lats, width), jnp.float32),
            pltpu.VMEM((n, mine, lats, width), jnp.float32),
            pltpu.VMEM((lats, width), jnp.int32),
            pltpu.VMEM((lats, width), jnp.float32),
            sem((mine, n)), sem((mine, n)), sem((mine, n)), sem((mine, n)),
            sem((mine,)), sem((mine,)), sem((pieces,)), sem((pieces,)),
        ],
        compiler_params=pltpu.CompilerParams(
            collective_id=0, has_side_effects=True, vmem_limit_bytes=24 << 20),
    )(*(pltpu.with_memory_space_constraint(a, pltpu.HBM)
        for a in (tracers, offsets, fraction, bin_class, thickness)))


def plan_kernel(chips, tiers, offsets_ref, table_ref, tier_ref, column):
    lats, width = column.shape
    bits = (2 * lats - 1).bit_length()

    @pl.loop(0, lats)
    def _(j):
        column[pl.ds(j, 1), :] = jnp.full((1, width), offsets_ref[j], jnp.int32)

    shift = column[...]
    lane = lax.broadcasted_iota(jnp.int32, shift.shape, 1)
    row = lax.broadcasted_iota(jnp.int32, shift.shape, 0)

    def flat(value):
        return jnp.sum(jnp.where(lane == row, value, 0).astype(jnp.float32), axis=0, keepdims=True).astype(jnp.int32)

    def count(chosen, axis):
        return jnp.sum(jnp.where(chosen, 1.0, 0.0), axis=axis, keepdims=True).astype(jnp.int32)

    def split(value):
        block = value // width
        chip = block // 2
        return value % width, chip, block % 2

    def onward(chip, by):
        moved = chip + by
        return jnp.where(moved >= chips, moved - chips, moved)

    rest, high, odd = split(shift)
    full, low = onward(high, odd), onward(high, 1)
    rest_of, high_of, odd_of = split(jnp.broadcast_to(flat(shift), shift.shape))
    full_of = onward(high_of, odd_of)
    real = lane < lats
    rank_full = count(real & (full_of == full) & (lane < row), 1)
    rank = count(real & (high_of == high) & ((rest_of < rest) | ((rest_of == rest) & (lane < row))), 1)

    fulls, highs, pairs, need = [], [], [], 0
    for d in range(chips):
        fulls.append(count(full == d, 0))
        highs.append(count(high == d, 0))
        either = count((low == d) & (rest < lane), 0) + count((high == d) & (rest > lane), 0)
        pairs.append(jnp.min(either.astype(jnp.float32), axis=1, keepdims=True).astype(jnp.int32))
    for d in range(1, chips):
        need = jnp.maximum(need, fulls[d] + highs[d] + highs[d - 1] - pairs[d])
    slots, tier = tiers[0], 0
    for before, after in zip(tiers, tiers[1:] + tiers[-1:]):
        slots = jnp.where(need > before, after, slots)
        tier = tier + jnp.where(need > before, 1, 0)

    def at(chip, values):
        picked = 0
        for d in range(chips):
            picked = picked + jnp.where(chip == d, values[d], 0)
        return picked

    full_slot = rank_full
    high_slot = at(high, fulls) + rank
    low_slot = at(low, fulls) + at(low, highs) + rank - at(low, pairs)
    own = 2 * lats

    def place(chip, slot, block):
        entry = jnp.where(chip == 0, -1, (chip - 1) * slots + slot)
        return entry, jnp.where(chip == 0, 2 * row + block, own + entry)

    full_entry, full_pool = place(full, full_slot, odd)
    high_entry, high_pool = place(high, high_slot, 1 - odd)
    low_entry, low_pool = place(low, low_slot, 1 - odd)
    for i, value in enumerate((full_pool, high_pool, low_pool, rest)):
        table_ref[pl.ds(i, 1), :] = flat(value)
    for w in range(table_ref.shape[0] - 4):
        entry = lane + w * width
        word = jnp.where(full_entry == entry, (width << (2 * bits)) + 2 * row + odd, 0)
        word += jnp.where(high_entry == entry, ((width - rest) << (2 * bits)) + 2 * row + 1 - odd, 0)
        word += jnp.where(low_entry == entry, (2 * row + 1 - odd) << bits, 0)
        table_ref[pl.ds(4 + w, 1), :] = jnp.sum(word.astype(jnp.float32), axis=0, keepdims=True).astype(jnp.int32)
    tier_ref[0] = jnp.max((tier + jnp.zeros((1, width), jnp.int32)).astype(jnp.float32)).astype(jnp.int32)


def direct_kernel(
    n, depth, slots, lats, levels, x_ref, table_hbm, fraction_hbm, class_hbm, thick_hbm, out_ref,
    table_ref, fraction_ref, class_ref, thick_ref, small, xin, xe, send, outb, zin, zout,
    own1, xs, xr, ss, rs, zs, zr, own2, hs, hr, *pools,
):
    width = x_ref.shape[1]
    chips = n // 2
    own = 2 * lats
    bits = (own - 1).bit_length()
    each = SUB // levels
    span = SUB * lats
    chunks = len(pools)
    late = chunks // 2
    me = lax.axis_index("lon")
    lev = lax.axis_index("lev")
    core = lax.rem(me, 2)
    partner = me + 1 - 2 * core

    def peer(d):
        return lax.rem(me + 2 * d, n)

    def part(c, side):
        return pl.ds(pl.multiple_of((side * chunks + c) * span, SUB), span)

    def own_in(c):
        return pltpu.make_async_copy(x_ref.at[part(c, core)], xin.at[2 * c + core], own1.at[c])

    def swap_in(c):
        return pltpu.make_async_remote_copy(
            src_ref=x_ref.at[part(c, 1 - core)], dst_ref=xin.at[2 * c + core],
            send_sem=xs.at[c], recv_sem=xr.at[c],
            device_id={"lon": partner}, device_id_type=pl.DeviceIdType.MESH,
        )

    def onward(c, d):
        return pltpu.make_async_remote_copy(
            src_ref=send.at[c, pl.ds((d - 1) * slots, slots)],
            dst_ref=pools[c].at[pl.ds(own + (d - 1) * slots, slots)],
            send_sem=ss.at[c, d], recv_sem=rs.at[c, d],
            device_id={"lon": peer(d)}, device_id_type=pl.DeviceIdType.MESH,
        )

    def downward(c):
        return pltpu.make_async_remote_copy(
            src_ref=zout.at[c], dst_ref=zin.at[c], send_sem=zs.at[c], recv_sem=zr.at[c],
            device_id={"lev": lax.rem(lev + 1, depth)}, device_id_type=pl.DeviceIdType.MESH,
        )

    def own_out(c):
        return pltpu.make_async_copy(outb.at[2 * c + core], out_ref.at[part(c, core)], own2.at[c])

    def swap_out(c):
        return pltpu.make_async_remote_copy(
            src_ref=outb.at[2 * c + 1 - core], dst_ref=out_ref.at[part(c, core)],
            send_sem=hs.at[c], recv_sem=hr.at[c],
            device_id={"lon": partner}, device_id_type=pl.DeviceIdType.MESH,
        )

    scalars = [
        pltpu.make_async_copy(source, held, small.at[i])
        for i, (source, held) in enumerate((
            (table_hbm, table_ref), (fraction_hbm, fraction_ref),
            (class_hbm, class_ref), (thick_hbm, thick_ref)))
    ]
    barrier = pltpu.get_barrier_semaphore()
    pl.semaphore_signal(barrier, inc=1, device_id={"lon": partner}, device_id_type=pl.DeviceIdType.MESH)
    for d in range(1, chips):
        pl.semaphore_signal(barrier, inc=1, device_id={"lon": peer(d)}, device_id_type=pl.DeviceIdType.MESH)
    for k in (1, depth - 1):
        pl.semaphore_signal(barrier, inc=1, device_id={"lev": lax.rem(lev + k, depth)},
                            device_id_type=pl.DeviceIdType.MESH)
    for c in range(chunks):
        own_in(c).start()
    for copy in scalars:
        copy.start()
    pl.semaphore_wait(barrier, chips + 2)
    for c in range(chunks):
        swap_in(c).start()
    for copy in scalars:
        copy.wait()

    def ratios(tracer):
        bin_class = jnp.full((SUB, width), class_ref[tracer // GROUPS], jnp.int32)
        speed = 0.5
        for b in range(3):
            speed = speed * jnp.where((bin_class & (1 << b)) != 0, 2.0 ** (1 << b), 1.0)
        return [speed / thick_ref[level] for level in range(levels)]

    lane = lax.broadcasted_iota(jnp.int32, (SUB, width), 1)

    def spread(c):
        @pl.loop(0, lats, unroll=4)
        def _(j):
            for side in (0, 1):
                value = xin[2 * c + side, pl.ds(j, SUB, stride=lats), :]
                xe[2 * j + side] = value
                pools[c][2 * j + side] = value

    def pack(c):
        @pl.loop(0, (chips - 1) * slots, unroll=4)
        def _(e):
            word = table_ref[4 + e // width, e % width]
            first = xe[word & (own - 1)]
            second = xe[(word >> bits) & (own - 1)]
            send[c, e] = jnp.where(lane < (word >> (2 * bits)), first, second)

        @pl.loop(1, chips)
        def _(d):
            onward(c, d).start()

    def unpack(c):
        pool = pools[c]

        @pl.loop(0, lats, unroll=2)
        def _(j):
            rest = table_ref[3, j]
            share = fraction_ref[j]
            full = pool[table_ref[0, j]]
            high = pool[table_ref[1, j]]
            low = pool[table_ref[2, j]]
            mixed = jnp.where(lane < width - rest, high, low)
            before = pltpu.roll(jnp.where(lane < width - 1 - rest, high, low), 1, axis=1)
            full_before = pltpu.roll(full, 1, axis=1)
            edge = lane == 0
            full = (1.0 - share) * full + share * jnp.where(edge, before, full_before)
            mixed = (1.0 - share) * mixed + share * jnp.where(edge, full_before, before)
            full = pltpu.roll(full, rest, axis=1)
            mixed = pltpu.roll(mixed, rest, axis=1)
            outb[2 * c, pl.ds(j, SUB, stride=lats), :] = jnp.where(lane < rest, mixed, full)
            outb[2 * c + 1, pl.ds(j, SUB, stride=lats), :] = jnp.where(lane < rest, full, mixed)

    def rows(tt, level, g):
        return pl.ds(pl.multiple_of((tt * levels + level) * lats + g * SUB, SUB), SUB)

    def bottom(side, tt, g):
        return pl.ds(pl.multiple_of((side * each + tt) * lats + g * SUB, SUB), SUB)

    def settle(held, c):
        for tt in range(each):
            ratio = ratios((core * chunks + c) * each + tt)
            keep = [1.0 / (1.0 + r) for r in ratio]
            carry = [r * k for r, k in zip(ratio, keep)]

            @pl.loop(0, lats // SUB)
            def _(g):
                for side in (0, 1):
                    value = None
                    for level in range(levels):
                        field = keep[level] * held[2 * c + side, rows(tt, level, g), :]
                        value = field if value is None else field + carry[level] * value
                        held[2 * c + side, rows(tt, level, g), :] = value
                    zout[c, bottom(side, tt, g), :] = value

    def sink(held, c):
        reaches = []
        for tt in range(each):
            reach = []
            for r in ratios((core * chunks + c) * each + tt):
                step = r / (1.0 + r)
                reach.append(reach[-1] * step if reach else step)
            reaches.append(reach)

        @pl.when(lev > 0)
        def _():
            downward(c).wait_recv()

            @pl.loop(0, lats // SUB)
            def _(g):
                for tt in range(each):
                    for side in (0, 1):
                        at = bottom(side, tt, g)
                        value = zout[c, at, :] + reaches[tt][-1] * zin[c, at, :]
                        zout[c, at, :] = value
                        held[2 * c + side, rows(tt, levels - 1, g), :] = value

        @pl.when(lev < depth - 1)
        def _():
            downward(c).start()

        @pl.when(lev > 0)
        def _():
            @pl.loop(0, lats // SUB)
            def _(g):
                for tt in range(each):
                    for side in (0, 1):
                        above = zin[c, bottom(side, tt, g), :]
                        for level in range(levels - 1):
                            held[2 * c + side, rows(tt, level, g), :] += reaches[tt][level] * above

    def arrive(c):
        own_in(c).wait()
        swap_in(c).wait_recv()

    for c in range(late):
        arrive(c)
        spread(c)
        pack(c)
    for c in range(late, chunks):
        arrive(c)
        settle(xin, c)
    for c in range(late, chunks):
        sink(xin, c)
        spread(c)
        pack(c)
    for c in range(chunks):
        @pl.loop(1, chips)
        def _(d):
            onward(c, d).wait_recv()

        unpack(c)
        if c < late:
            settle(outb, c)
            sink(outb, c)
        own_out(c).start()
        swap_out(c).start()

    @pl.when(lev < depth - 1)
    def _():
        @pl.loop(0, chunks)
        def _(c):
            downward(c).wait_send()

    for c in range(chunks):
        swap_in(c).wait_send()

        @pl.loop(1, chips)
        def _(d):
            onward(c, d).wait_send()

        own_out(c).wait()
        swap_out(c).wait()


def in_hbm(arrays):
    return tuple(pltpu.with_memory_space_constraint(a, pltpu.HBM) for a in arrays)


def make_plan(offsets, chips, width, tiers):
    lats = offsets.shape[0]
    words = -(-(chips - 1) * tiers[-1] // width)
    return pl.pallas_call(
        functools.partial(plan_kernel, chips, tiers),
        out_shape=(jax.ShapeDtypeStruct((4 + words, width), jnp.int32), jax.ShapeDtypeStruct((1,), jnp.int32)),
        in_specs=[pl.BlockSpec(memory_space=pltpu.SMEM)],
        out_specs=(pl.BlockSpec(memory_space=pltpu.VMEM), pl.BlockSpec(memory_space=pltpu.SMEM)),
        scratch_shapes=[pltpu.VMEM((lats, width), jnp.int32)],
    )(offsets)


def direct(slots, identity, tracers, table, fraction, bin_class, thickness):
    count, levels, lats, width = tracers.shape
    n = lax.axis_size("lon")
    depth = lax.axis_size("lev")
    chips = n // 2
    chunks = count * levels // (2 * SUB)
    span = SUB * lats
    entries = (chips - 1) * slots
    hbm = pl.BlockSpec(memory_space=pltpu.HBM)
    held = [pltpu.SMEM(a.shape, a.dtype) for a in (table, fraction, bin_class, thickness)]
    sem = pltpu.SemaphoreType.DMA
    edge = 2 * (SUB // levels) * lats
    out = pl.pallas_call(
        functools.partial(direct_kernel, n, depth, slots, lats, levels),
        out_shape=jax.ShapeDtypeStruct((count * levels * lats, width), jnp.float32),
        in_specs=[hbm] * 5,
        out_specs=pl.BlockSpec(memory_space=pl.ANY),
        scratch_shapes=[
            *held, sem((4,)),
            pltpu.VMEM((2 * chunks, span, width), jnp.float32),
            pltpu.VMEM((2 * lats, SUB, width), jnp.float32),
            pltpu.VMEM((chunks, entries, SUB, width), jnp.float32),
            pltpu.VMEM((2 * chunks, span, width), jnp.float32),
            pltpu.VMEM((chunks, edge, width), jnp.float32),
            pltpu.VMEM((chunks, edge, width), jnp.float32),
            sem((chunks,)), sem((chunks,)), sem((chunks,)),
            sem((chunks, chips)), sem((chunks, chips)), sem((chunks,)), sem((chunks,)),
            sem((chunks,)), sem((chunks,)), sem((chunks,)),
            *[pltpu.VMEM((2 * lats + entries, SUB, width), jnp.float32)] * chunks,
        ],
        compiler_params=pltpu.CompilerParams(
            collective_id=identity, has_side_effects=True, vmem_limit_bytes=44 << 20),
    )(*in_hbm((tracers.reshape(-1, width), table, fraction, bin_class, thickness)))
    return out.reshape(tracers.shape)


def on_device(tracers, offsets, fraction, bin_class, thickness):
    count, levels, lats, width = tracers.shape
    n = lax.axis_size("lon")
    if width != 128 or lats != 64 or n % 2 or n < 4 or SUB % levels or count * levels % (2 * SUB):
        return by_tracer(tracers, offsets, fraction, bin_class, thickness)
    tiers = []
    for share in SHARES:
        slots = -(-share * lats // (64 * n // 2)) * 4
        if slots not in tiers:
            tiers.append(slots)
    table, tier = make_plan(offsets, n // 2, width, tiers)
    ways = [
        functools.partial(lambda slots, i, x, o, t, f, b, h: direct(slots, i, x, t, f, b, h), slots, i + 1)
        for i, slots in enumerate(tiers)
    ]
    ways.append(lambda x, o, t, f, b, h: by_tracer(x, o, f, b, h))
    return lax.switch(tier[0], ways, tracers, offsets, table, fraction, bin_class, thickness)


def solution(mesh):
    in_specs = (P(None, "lev", None, "lon"), P(), P(), P(), P("lev"))
    out_specs = P(None, "lev", None, "lon")
    return jax.shard_map(
        on_device, mesh=mesh, in_specs=in_specs, out_specs=out_specs, check_vma=False
    )
```

```python
import functools

import jax
import jax.numpy as jnp
from jax import lax
from jax.experimental import pallas as pl
from jax.experimental.pallas import tpu as pltpu
from jax.sharding import PartitionSpec as P

GROUPS = 4
SUB = 8
PIECES = 8
HOLD = 3
SHARES = (36, 40, 44, 48, 56)


def exchange_kernel(
    n, depth, x_ref, offsets_hbm, fraction_hbm, class_hbm, thick_hbm, out_ref,
    offsets_ref, fraction_ref, class_ref, thick_ref, small, recv, obuf, zin, row_ref, share_ref, s1, r1, s2, r2, own1, own2, zs, zr,
):
    tracers, levels, lats, width = x_ref.shape
    mine = tracers // n
    halves = max(1, min(PIECES // mine, lats // SUB))
    rows_of = lats // halves
    me = lax.axis_index("lon")
    lev = lax.axis_index("lev")

    def at(c):
        return c // halves, pl.ds(pl.multiple_of((c % halves) * rows_of, SUB), rows_of)

    def peer(k):
        return lax.rem(me + k, n)

    def outward(tt, k):
        return pltpu.make_async_remote_copy(
            src_ref=x_ref.at[peer(k) * mine + tt],
            dst_ref=recv.at[me, tt],
            send_sem=s1.at[tt, k], recv_sem=r1.at[tt, k],
            device_id={"lon": peer(k)}, device_id_type=pl.DeviceIdType.MESH,
        )

    def homeward(tt, k):
        return pltpu.make_async_remote_copy(
            src_ref=obuf.at[peer(k), tt],
            dst_ref=out_ref.at[me * mine + tt],
            send_sem=s2.at[tt, k], recv_sem=r2.at[tt, k],
            device_id={"lon": peer(k)}, device_id_type=pl.DeviceIdType.MESH,
        )

    def downward(c):
        tt, rows = at(c)
        return pltpu.make_async_remote_copy(
            src_ref=obuf.at[:, tt, levels - 1, rows, :],
            dst_ref=zin.at[:, tt, rows, :],
            send_sem=zs.at[c], recv_sem=zr.at[c],
            device_id={"lev": lax.rem(lev + 1, depth)}, device_id_type=pl.DeviceIdType.MESH,
        )

    def own_in(tt):
        return pltpu.make_async_copy(x_ref.at[me * mine + tt], recv.at[me, tt], own1.at[tt])

    def own_out(tt):
        return pltpu.make_async_copy(obuf.at[me, tt], out_ref.at[me * mine + tt], own2.at[tt])

    scalars = [
        pltpu.make_async_copy(source, held, small.at[i])
        for i, (source, held) in enumerate((
            (offsets_hbm, offsets_ref), (fraction_hbm, fraction_ref),
            (class_hbm, class_ref), (thick_hbm, thick_ref)))
    ]
    for copy in scalars:
        copy.start()

    barrier = pltpu.get_barrier_semaphore()
    for k in range(1, n):
        pl.semaphore_signal(barrier, inc=1, device_id={"lon": peer(k)},
                            device_id_type=pl.DeviceIdType.MESH)
    for k in (1, depth - 1):
        pl.semaphore_signal(barrier, inc=1, device_id={"lev": lax.rem(lev + k, depth)},
                            device_id_type=pl.DeviceIdType.MESH)
    pl.semaphore_wait(barrier, n + 1)

    count = mine * halves

    @pl.loop(0, mine)
    def _(tt):
        @pl.loop(1, n)
        def _(k):
            outward(tt, k).start()

        own_in(tt).start()

    for copy in scalars:
        copy.wait()

    @pl.loop(0, lats)
    def _(j):
        shift = jnp.full((1, width), offsets_ref[j], jnp.int32)
        row_ref[pl.ds(j, 1), :] = shift
        share_ref[pl.ds(j, 1), :] = jnp.full((1, width), fraction_ref[j], jnp.float32)

    def ratios(tracer):
        bin_class = jnp.full((SUB, width), class_ref[tracer // GROUPS], jnp.int32)
        speed = 0.5
        for b in range(3):
            speed = speed * jnp.where((bin_class & (1 << b)) != 0, 2.0 ** (1 << b), 1.0)
        return [speed / thick_ref[level] for level in range(levels)]

    lane = lax.broadcasted_iota(jnp.int32, (SUB, width), 1)

    def behind(value, by):
        by %= n
        if by == 0:
            return value
        return jnp.concatenate([value[n - by:], value[:n - by]], axis=0)

    def turn(c):
        tt = c // halves
        base = (c % halves) * rows_of
        ratio = ratios(me * mine + tt)
        keep = [1.0 / (1.0 + r) for r in ratio]
        carry = [r * k for r, k in zip(ratio, keep)]

        @pl.when(c % halves == 0)
        def _():
            own_in(tt).wait()

            @pl.loop(1, n)
            def _(k):
                outward(tt, k).wait_recv()

        @pl.loop(0, rows_of // SUB)
        def _(g):
            rows = pl.ds(pl.multiple_of(base + g * SUB, SUB), SUB)
            shift = row_ref[rows, :]
            remainder = lax.rem(shift, width)
            quotient = lax.div(shift, width)
            share = share_ref[rows, :]
            fine = [(remainder & (1 << b)) != 0 for b in range((width - 1).bit_length())]
            coarse = [(quotient & (1 << b)) != 0 for b in range((n - 1).bit_length())]
            same_block = lane >= remainder
            first_lane = lane == 0
            value = None
            for level in range(levels):
                field = recv[:, tt, level, rows, :]
                turned = pltpu.roll(field, 1, axis=2)
                left = jnp.where(first_lane[None], behind(turned, 1), turned)
                field = (1.0 - share)[None] * field + share[None] * left
                for b, chosen in enumerate(fine):
                    field = jnp.where(chosen[None], pltpu.roll(field, 1 << b, axis=2), field)
                field = jnp.where(same_block[None], field, behind(field, 1))
                for b, chosen in enumerate(coarse):
                    field = jnp.where(chosen[None], behind(field, 1 << b), field)
                field = keep[level][None] * field
                value = field if value is None else field + carry[level][None] * value
                obuf[:, tt, level, rows, :] = value

    def settle(c):
        tt = c // halves
        base = (c % halves) * rows_of
        reach = []
        for r in ratios(me * mine + tt):
            step = r / (1.0 + r)
            reach.append(reach[-1] * step if reach else step)

        def add_above(level):
            @pl.loop(0, rows_of // SUB)
            def _(g):
                rows = pl.ds(pl.multiple_of(base + g * SUB, SUB), SUB)
                obuf[:, tt, level, rows, :] += reach[level][None] * zin[:, tt, rows, :]

        @pl.when(lev > 0)
        def _():
            downward(c).wait_recv()
            add_above(levels - 1)

        @pl.when(lev < depth - 1)
        def _():
            downward(c).start()

        @pl.when(lev > 0)
        def _():
            for level in range(levels - 1):
                add_above(level)

    def send_home(tt):
        @pl.loop(1, n)
        def _(k):
            homeward(tt, k).start()

        own_out(tt).start()

    hold = min(HOLD, count - 1)

    @pl.loop(0, count + depth - 1)
    def _(i):
        @pl.when(i < count)
        def _():
            turn(i)

        done = i - lev

        @pl.when((done >= 0) & (done < count))
        def _():
            settle(done)

        @pl.when((done >= 0) & (done < count) & (done % halves == halves - 1) & (i > hold))
        def _():
            send_home(done // halves)

        @pl.when(i == hold)
        def _():
            @pl.loop(0, mine)
            def _(tt):
                @pl.when((tt + 1) * halves - 1 <= done)
                def _():
                    send_home(tt)

    @pl.when(lev < depth - 1)
    def _():
        @pl.loop(0, count)
        def _(c):
            downward(c).wait_send()

    @pl.loop(0, mine)
    def _(tt):
        own_out(tt).wait()

        @pl.loop(1, n)
        def _(k):
            outward(tt, k).wait_send()
            homeward(tt, k).wait()


def by_tracer(tracers, offsets, fraction, bin_class, thickness):
    count, levels, lats, width = tracers.shape
    n = lax.axis_size("lon")
    depth = lax.axis_size("lev")
    mine = count // n
    pieces = mine * max(1, min(PIECES // mine, lats // SUB))
    hbm = pl.BlockSpec(memory_space=pltpu.HBM)
    held = [pltpu.SMEM(a.shape, a.dtype) for a in (offsets, fraction, bin_class, thickness)]
    sem = pltpu.SemaphoreType.DMA
    return pl.pallas_call(
        functools.partial(exchange_kernel, n, depth),
        out_shape=jax.ShapeDtypeStruct(tracers.shape, jnp.float32),
        in_specs=[hbm] * 5,
        out_specs=pl.BlockSpec(memory_space=pl.ANY),
        scratch_shapes=[
            *held, sem((4,)),
            pltpu.VMEM((n, mine, levels, lats, width), jnp.float32),
            pltpu.VMEM((n, mine, levels, lats, width), jnp.float32),
            pltpu.VMEM((n, mine, lats, width), jnp.float32),
            pltpu.VMEM((lats, width), jnp.int32),
            pltpu.VMEM((lats, width), jnp.float32),
            sem((mine, n)), sem((mine, n)), sem((mine, n)), sem((mine, n)),
            sem((mine,)), sem((mine,)), sem((pieces,)), sem((pieces,)),
        ],
        compiler_params=pltpu.CompilerParams(
            collective_id=0, has_side_effects=True, vmem_limit_bytes=24 << 20),
    )(*(pltpu.with_memory_space_constraint(a, pltpu.HBM)
        for a in (tracers, offsets, fraction, bin_class, thickness)))


def plan_kernel(chips, tiers, offsets_ref, table_ref, tier_ref, column):
    lats, width = column.shape
    bits = (2 * lats - 1).bit_length()

    @pl.loop(0, lats)
    def _(j):
        column[pl.ds(j, 1), :] = jnp.full((1, width), offsets_ref[j], jnp.int32)

    shift = column[...]
    lane = lax.broadcasted_iota(jnp.int32, shift.shape, 1)
    row = lax.broadcasted_iota(jnp.int32, shift.shape, 0)

    def flat(value):
        return jnp.sum(jnp.where(lane == row, value, 0).astype(jnp.float32), axis=0, keepdims=True).astype(jnp.int32)

    def count(chosen, axis):
        return jnp.sum(jnp.where(chosen, 1.0, 0.0), axis=axis, keepdims=True).astype(jnp.int32)

    def split(value):
        block = value // width
        chip = block // 2
        return value % width, chip, block % 2

    def onward(chip, by):
        moved = chip + by
        return jnp.where(moved >= chips, moved - chips, moved)

    rest, high, odd = split(shift)
    full, low = onward(high, odd), onward(high, 1)
    rest_of, high_of, odd_of = split(jnp.broadcast_to(flat(shift), shift.shape))
    full_of = onward(high_of, odd_of)
    real = lane < lats
    rank_full = count(real & (full_of == full) & (lane < row), 1)
    rank = count(real & (high_of == high) & ((rest_of < rest) | ((rest_of == rest) & (lane < row))), 1)

    fulls, highs, pairs, need = [], [], [], 0
    for d in range(chips):
        fulls.append(count(full == d, 0))
        highs.append(count(high == d, 0))
        either = count((low == d) & (rest < lane), 0) + count((high == d) & (rest > lane), 0)
        pairs.append(jnp.min(either.astype(jnp.float32), axis=1, keepdims=True).astype(jnp.int32))
    for d in range(1, chips):
        need = jnp.maximum(need, fulls[d] + highs[d] + highs[d - 1] - pairs[d])
    slots, tier = tiers[0], 0
    for before, after in zip(tiers, tiers[1:] + tiers[-1:]):
        slots = jnp.where(need > before, after, slots)
        tier = tier + jnp.where(need > before, 1, 0)

    def at(chip, values):
        picked = 0
        for d in range(chips):
            picked = picked + jnp.where(chip == d, values[d], 0)
        return picked

    full_slot = rank_full
    high_slot = at(high, fulls) + rank
    low_slot = at(low, fulls) + at(low, highs) + rank - at(low, pairs)
    own = 2 * lats

    def place(chip, slot, block):
        entry = jnp.where(chip == 0, -1, (chip - 1) * slots + slot)
        return entry, jnp.where(chip == 0, 2 * row + block, own + entry)

    full_entry, full_pool = place(full, full_slot, odd)
    high_entry, high_pool = place(high, high_slot, 1 - odd)
    low_entry, low_pool = place(low, low_slot, 1 - odd)
    for i, value in enumerate((full_pool, high_pool, low_pool, rest)):
        table_ref[pl.ds(i, 1), :] = flat(value)
    for w in range(table_ref.shape[0] - 4):
        entry = lane + w * width
        word = jnp.where(full_entry == entry, (width << (2 * bits)) + 2 * row + odd, 0)
        word += jnp.where(high_entry == entry, ((width - rest) << (2 * bits)) + 2 * row + 1 - odd, 0)
        word += jnp.where(low_entry == entry, (2 * row + 1 - odd) << bits, 0)
        table_ref[pl.ds(4 + w, 1), :] = jnp.sum(word.astype(jnp.float32), axis=0, keepdims=True).astype(jnp.int32)
    tier_ref[0] = jnp.max((tier + jnp.zeros((1, width), jnp.int32)).astype(jnp.float32)).astype(jnp.int32)


def direct_kernel(
    n, depth, slots, lats, levels, x_ref, table_hbm, fraction_hbm, class_hbm, thick_hbm, out_ref,
    table_ref, fraction_ref, class_ref, thick_ref, small, xin, xe, send, outb, zin, zout,
    own1, xs, xr, ss, rs, zs, zr, own2, hs, hr, *pools,
):
    width = x_ref.shape[1]
    chips = n // 2
    own = 2 * lats
    bits = (own - 1).bit_length()
    each = SUB // levels
    span = SUB * lats
    chunks = len(pools)
    late = chunks // 2
    me = lax.axis_index("lon")
    lev = lax.axis_index("lev")
    core = lax.rem(me, 2)
    partner = me + 1 - 2 * core

    def peer(d):
        return lax.rem(me + 2 * d, n)

    def part(c, side):
        return pl.ds(pl.multiple_of((side * chunks + c) * span, SUB), span)

    def own_in(c):
        return pltpu.make_async_copy(x_ref.at[part(c, core)], xin.at[2 * c + core], own1.at[c])

    def swap_in(c):
        return pltpu.make_async_remote_copy(
            src_ref=x_ref.at[part(c, 1 - core)], dst_ref=xin.at[2 * c + core],
            send_sem=xs.at[c], recv_sem=xr.at[c],
            device_id={"lon": partner}, device_id_type=pl.DeviceIdType.MESH,
        )

    def onward(c, d):
        return pltpu.make_async_remote_copy(
            src_ref=send.at[c, pl.ds((d - 1) * slots, slots)],
            dst_ref=pools[c].at[pl.ds(own + (d - 1) * slots, slots)],
            send_sem=ss.at[c, d], recv_sem=rs.at[c, d],
            device_id={"lon": peer(d)}, device_id_type=pl.DeviceIdType.MESH,
        )

    def downward(c):
        return pltpu.make_async_remote_copy(
            src_ref=zout.at[c], dst_ref=zin.at[c], send_sem=zs.at[c], recv_sem=zr.at[c],
            device_id={"lev": lax.rem(lev + 1, depth)}, device_id_type=pl.DeviceIdType.MESH,
        )

    def own_out(c):
        return pltpu.make_async_copy(outb.at[2 * c + core], out_ref.at[part(c, core)], own2.at[c])

    def swap_out(c):
        return pltpu.make_async_remote_copy(
            src_ref=outb.at[2 * c + 1 - core], dst_ref=out_ref.at[part(c, core)],
            send_sem=hs.at[c], recv_sem=hr.at[c],
            device_id={"lon": partner}, device_id_type=pl.DeviceIdType.MESH,
        )

    scalars = [
        pltpu.make_async_copy(source, held, small.at[i])
        for i, (source, held) in enumerate((
            (table_hbm, table_ref), (fraction_hbm, fraction_ref),
            (class_hbm, class_ref), (thick_hbm, thick_ref)))
    ]
    barrier = pltpu.get_barrier_semaphore()
    pl.semaphore_signal(barrier, inc=1, device_id={"lon": partner}, device_id_type=pl.DeviceIdType.MESH)
    for d in range(1, chips):
        pl.semaphore_signal(barrier, inc=1, device_id={"lon": peer(d)}, device_id_type=pl.DeviceIdType.MESH)
    for k in (1, depth - 1):
        pl.semaphore_signal(barrier, inc=1, device_id={"lev": lax.rem(lev + k, depth)},
                            device_id_type=pl.DeviceIdType.MESH)
    for c in range(chunks):
        own_in(c).start()
    for copy in scalars:
        copy.start()
    pl.semaphore_wait(barrier, chips + 2)
    for c in range(chunks):
        swap_in(c).start()
    for copy in scalars:
        copy.wait()

    def ratios(tracer):
        bin_class = jnp.full((SUB, width), class_ref[tracer // GROUPS], jnp.int32)
        speed = 0.5
        for b in range(3):
            speed = speed * jnp.where((bin_class & (1 << b)) != 0, 2.0 ** (1 << b), 1.0)
        return [speed / thick_ref[level] for level in range(levels)]

    lane = lax.broadcasted_iota(jnp.int32, (SUB, width), 1)

    def spread(c):
        @pl.loop(0, lats, unroll=8)
        def _(j):
            for side in (0, 1):
                value = xin[2 * c + side, pl.ds(j, SUB, stride=lats), :]
                xe[2 * j + side] = value
                pools[c][2 * j + side] = value

    def pack(c):
        @pl.loop(0, (chips - 1) * slots, unroll=12)
        def _(e):
            word = table_ref[4 + e // width, e % width]
            first = xe[word & (own - 1)]
            second = xe[(word >> bits) & (own - 1)]
            send[c, e] = jnp.where(lane < (word >> (2 * bits)), first, second)

        @pl.loop(1, chips)
        def _(d):
            onward(c, d).start()

    def unpack(c):
        pool = pools[c]

        @pl.loop(0, lats, unroll=16)
        def _(j):
            rest = table_ref[3, j]
            share = fraction_ref[j]
            full = pool[table_ref[0, j]]
            high = pool[table_ref[1, j]]
            low = pool[table_ref[2, j]]
            mixed = jnp.where(lane < width - rest, high, low)
            before = pltpu.roll(jnp.where(lane < width - 1 - rest, high, low), 1, axis=1)
            full_before = pltpu.roll(full, 1, axis=1)
            edge = lane == 0
            full = (1.0 - share) * full + share * jnp.where(edge, before, full_before)
            mixed = (1.0 - share) * mixed + share * jnp.where(edge, full_before, before)
            full = pltpu.roll(full, rest, axis=1)
            mixed = pltpu.roll(mixed, rest, axis=1)
            outb[2 * c, pl.ds(j, SUB, stride=lats), :] = jnp.where(lane < rest, mixed, full)
            outb[2 * c + 1, pl.ds(j, SUB, stride=lats), :] = jnp.where(lane < rest, full, mixed)

    def rows(tt, level, g):
        return pl.ds(pl.multiple_of((tt * levels + level) * lats + g * SUB, SUB), SUB)

    def bottom(side, tt, g):
        return pl.ds(pl.multiple_of((side * each + tt) * lats + g * SUB, SUB), SUB)

    def settle(held, c):
        for tt in range(each):
            ratio = ratios((core * chunks + c) * each + tt)
            keep = [1.0 / (1.0 + r) for r in ratio]
            carry = [r * k for r, k in zip(ratio, keep)]

            @pl.loop(0, lats // SUB)
            def _(g):
                for side in (0, 1):
                    value = None
                    for level in range(levels):
                        field = keep[level] * held[2 * c + side, rows(tt, level, g), :]
                        value = field if value is None else field + carry[level] * value
                        held[2 * c + side, rows(tt, level, g), :] = value
                    zout[c, bottom(side, tt, g), :] = value

    def sink(held, c):
        reaches = []
        for tt in range(each):
            reach = []
            for r in ratios((core * chunks + c) * each + tt):
                step = r / (1.0 + r)
                reach.append(reach[-1] * step if reach else step)
            reaches.append(reach)

        @pl.when(lev > 0)
        def _():
            downward(c).wait_recv()

            @pl.loop(0, lats // SUB)
            def _(g):
                for tt in range(each):
                    for side in (0, 1):
                        at = bottom(side, tt, g)
                        value = zout[c, at, :] + reaches[tt][-1] * zin[c, at, :]
                        zout[c, at, :] = value
                        held[2 * c + side, rows(tt, levels - 1, g), :] = value

        @pl.when(lev < depth - 1)
        def _():
            downward(c).start()

        @pl.when(lev > 0)
        def _():
            @pl.loop(0, lats // SUB)
            def _(g):
                for tt in range(each):
                    for side in (0, 1):
                        above = zin[c, bottom(side, tt, g), :]
                        for level in range(levels - 1):
                            held[2 * c + side, rows(tt, level, g), :] += reaches[tt][level] * above

    def arrive(c):
        own_in(c).wait()
        swap_in(c).wait_recv()

    for c in range(late):
        arrive(c)
        spread(c)
        pack(c)
    for c in range(late, chunks):
        arrive(c)
        settle(xin, c)
    for c in range(late, chunks):
        sink(xin, c)
        spread(c)
        pack(c)
    for c in range(chunks):
        @pl.loop(1, chips)
        def _(d):
            onward(c, d).wait_recv()

        unpack(c)
        if c < late:
            settle(outb, c)
            sink(outb, c)
        own_out(c).start()
        swap_out(c).start()

    @pl.when(lev < depth - 1)
    def _():
        @pl.loop(0, chunks)
        def _(c):
            downward(c).wait_send()

    for c in range(chunks):
        swap_in(c).wait_send()

        @pl.loop(1, chips)
        def _(d):
            onward(c, d).wait_send()

        own_out(c).wait()
        swap_out(c).wait()


def in_hbm(arrays):
    return tuple(pltpu.with_memory_space_constraint(a, pltpu.HBM) for a in arrays)


def make_plan(offsets, chips, width, tiers):
    lats = offsets.shape[0]
    words = -(-(chips - 1) * tiers[-1] // width)
    return pl.pallas_call(
        functools.partial(plan_kernel, chips, tiers),
        out_shape=(jax.ShapeDtypeStruct((4 + words, width), jnp.int32), jax.ShapeDtypeStruct((1,), jnp.int32)),
        in_specs=[pl.BlockSpec(memory_space=pltpu.SMEM)],
        out_specs=(pl.BlockSpec(memory_space=pltpu.VMEM), pl.BlockSpec(memory_space=pltpu.SMEM)),
        scratch_shapes=[pltpu.VMEM((lats, width), jnp.int32)],
    )(offsets)


def direct(slots, identity, tracers, table, fraction, bin_class, thickness):
    count, levels, lats, width = tracers.shape
    n = lax.axis_size("lon")
    depth = lax.axis_size("lev")
    chips = n // 2
    chunks = count * levels // (2 * SUB)
    span = SUB * lats
    entries = (chips - 1) * slots
    hbm = pl.BlockSpec(memory_space=pltpu.HBM)
    held = [pltpu.SMEM(a.shape, a.dtype) for a in (table, fraction, bin_class, thickness)]
    sem = pltpu.SemaphoreType.DMA
    edge = 2 * (SUB // levels) * lats
    out = pl.pallas_call(
        functools.partial(direct_kernel, n, depth, slots, lats, levels),
        out_shape=jax.ShapeDtypeStruct((count * levels * lats, width), jnp.float32),
        in_specs=[hbm] * 5,
        out_specs=pl.BlockSpec(memory_space=pl.ANY),
        scratch_shapes=[
            *held, sem((4,)),
            pltpu.VMEM((2 * chunks, span, width), jnp.float32),
            pltpu.VMEM((2 * lats, SUB, width), jnp.float32),
            pltpu.VMEM((chunks, entries, SUB, width), jnp.float32),
            pltpu.VMEM((2 * chunks, span, width), jnp.float32),
            pltpu.VMEM((chunks, edge, width), jnp.float32),
            pltpu.VMEM((chunks, edge, width), jnp.float32),
            sem((chunks,)), sem((chunks,)), sem((chunks,)),
            sem((chunks, chips)), sem((chunks, chips)), sem((chunks,)), sem((chunks,)),
            sem((chunks,)), sem((chunks,)), sem((chunks,)),
            *[pltpu.VMEM((2 * lats + entries, SUB, width), jnp.float32)] * chunks,
        ],
        compiler_params=pltpu.CompilerParams(
            collective_id=identity, has_side_effects=True, vmem_limit_bytes=44 << 20),
    )(*in_hbm((tracers.reshape(-1, width), table, fraction, bin_class, thickness)))
    return out.reshape(tracers.shape)


def on_device(tracers, offsets, fraction, bin_class, thickness):
    count, levels, lats, width = tracers.shape
    n = lax.axis_size("lon")
    if width != 128 or lats != 64 or n % 2 or n < 4 or SUB % levels or count * levels % (2 * SUB):
        return by_tracer(tracers, offsets, fraction, bin_class, thickness)
    tiers = []
    for share in SHARES:
        slots = -(-share * lats // (64 * n // 2)) * 4
        if slots not in tiers:
            tiers.append(slots)
    table, tier = make_plan(offsets, n // 2, width, tiers)
    ways = [
        functools.partial(lambda slots, i, x, o, t, f, b, h: direct(slots, i, x, t, f, b, h), slots, i + 1)
        for i, slots in enumerate(tiers)
    ]
    ways.append(lambda x, o, t, f, b, h: by_tracer(x, o, f, b, h))
    return lax.switch(tier[0], ways, tracers, offsets, table, fraction, bin_class, thickness)


def solution(mesh):
    in_specs = (P(None, "lev", None, "lon"), P(), P(), P(), P("lev"))
    out_specs = P(None, "lev", None, "lon")
    return jax.shard_map(
        on_device, mesh=mesh, in_specs=in_specs, out_specs=out_specs, check_vma=False
    )
```

```python
import functools

import jax
import jax.numpy as jnp
from jax import lax
from jax.experimental import pallas as pl
from jax.experimental.pallas import tpu as pltpu
from jax.sharding import PartitionSpec as P

GROUPS = 4
SUB = 8
PIECES = 8
HOLD = 3
SHARES = (34, 36, 38, 40, 44, 50)
SEGMENTS = 5


def exchange_kernel(
    n, depth, x_ref, offsets_hbm, fraction_hbm, class_hbm, thick_hbm, out_ref,
    offsets_ref, fraction_ref, class_ref, thick_ref, small, recv, obuf, zin, row_ref, share_ref, s1, r1, s2, r2, own1, own2, zs, zr,
):
    tracers, levels, lats, width = x_ref.shape
    mine = tracers // n
    halves = max(1, min(PIECES // mine, lats // SUB))
    rows_of = lats // halves
    me = lax.axis_index("lon")
    lev = lax.axis_index("lev")

    def at(c):
        return c // halves, pl.ds(pl.multiple_of((c % halves) * rows_of, SUB), rows_of)

    def peer(k):
        return lax.rem(me + k, n)

    def outward(tt, k):
        return pltpu.make_async_remote_copy(
            src_ref=x_ref.at[peer(k) * mine + tt],
            dst_ref=recv.at[me, tt],
            send_sem=s1.at[tt, k], recv_sem=r1.at[tt, k],
            device_id={"lon": peer(k)}, device_id_type=pl.DeviceIdType.MESH,
        )

    def homeward(tt, k):
        return pltpu.make_async_remote_copy(
            src_ref=obuf.at[peer(k), tt],
            dst_ref=out_ref.at[me * mine + tt],
            send_sem=s2.at[tt, k], recv_sem=r2.at[tt, k],
            device_id={"lon": peer(k)}, device_id_type=pl.DeviceIdType.MESH,
        )

    def downward(c):
        tt, rows = at(c)
        return pltpu.make_async_remote_copy(
            src_ref=obuf.at[:, tt, levels - 1, rows, :],
            dst_ref=zin.at[:, tt, rows, :],
            send_sem=zs.at[c], recv_sem=zr.at[c],
            device_id={"lev": lax.rem(lev + 1, depth)}, device_id_type=pl.DeviceIdType.MESH,
        )

    def own_in(tt):
        return pltpu.make_async_copy(x_ref.at[me * mine + tt], recv.at[me, tt], own1.at[tt])

    def own_out(tt):
        return pltpu.make_async_copy(obuf.at[me, tt], out_ref.at[me * mine + tt], own2.at[tt])

    scalars = [
        pltpu.make_async_copy(source, held, small.at[i])
        for i, (source, held) in enumerate((
            (offsets_hbm, offsets_ref), (fraction_hbm, fraction_ref),
            (class_hbm, class_ref), (thick_hbm, thick_ref)))
    ]
    for copy in scalars:
        copy.start()

    barrier = pltpu.get_barrier_semaphore()
    for k in range(1, n):
        pl.semaphore_signal(barrier, inc=1, device_id={"lon": peer(k)},
                            device_id_type=pl.DeviceIdType.MESH)
    for k in (1, depth - 1):
        pl.semaphore_signal(barrier, inc=1, device_id={"lev": lax.rem(lev + k, depth)},
                            device_id_type=pl.DeviceIdType.MESH)
    pl.semaphore_wait(barrier, n + 1)

    count = mine * halves

    @pl.loop(0, mine)
    def _(tt):
        @pl.loop(1, n)
        def _(k):
            outward(tt, k).start()

        own_in(tt).start()

    for copy in scalars:
        copy.wait()

    @pl.loop(0, lats)
    def _(j):
        shift = jnp.full((1, width), offsets_ref[j], jnp.int32)
        row_ref[pl.ds(j, 1), :] = shift
        share_ref[pl.ds(j, 1), :] = jnp.full((1, width), fraction_ref[j], jnp.float32)

    def ratios(tracer):
        bin_class = jnp.full((SUB, width), class_ref[tracer // GROUPS], jnp.int32)
        speed = 0.5
        for b in range(3):
            speed = speed * jnp.where((bin_class & (1 << b)) != 0, 2.0 ** (1 << b), 1.0)
        return [speed / thick_ref[level] for level in range(levels)]

    lane = lax.broadcasted_iota(jnp.int32, (SUB, width), 1)

    def behind(value, by):
        by %= n
        if by == 0:
            return value
        return jnp.concatenate([value[n - by:], value[:n - by]], axis=0)

    def turn(c):
        tt = c // halves
        base = (c % halves) * rows_of
        ratio = ratios(me * mine + tt)
        keep = [1.0 / (1.0 + r) for r in ratio]
        carry = [r * k for r, k in zip(ratio, keep)]

        @pl.when(c % halves == 0)
        def _():
            own_in(tt).wait()

            @pl.loop(1, n)
            def _(k):
                outward(tt, k).wait_recv()

        @pl.loop(0, rows_of // SUB)
        def _(g):
            rows = pl.ds(pl.multiple_of(base + g * SUB, SUB), SUB)
            shift = row_ref[rows, :]
            remainder = lax.rem(shift, width)
            quotient = lax.div(shift, width)
            share = share_ref[rows, :]
            fine = [(remainder & (1 << b)) != 0 for b in range((width - 1).bit_length())]
            coarse = [(quotient & (1 << b)) != 0 for b in range((n - 1).bit_length())]
            same_block = lane >= remainder
            first_lane = lane == 0
            value = None
            for level in range(levels):
                field = recv[:, tt, level, rows, :]
                turned = pltpu.roll(field, 1, axis=2)
                left = jnp.where(first_lane[None], behind(turned, 1), turned)
                field = (1.0 - share)[None] * field + share[None] * left
                for b, chosen in enumerate(fine):
                    field = jnp.where(chosen[None], pltpu.roll(field, 1 << b, axis=2), field)
                field = jnp.where(same_block[None], field, behind(field, 1))
                for b, chosen in enumerate(coarse):
                    field = jnp.where(chosen[None], behind(field, 1 << b), field)
                field = keep[level][None] * field
                value = field if value is None else field + carry[level][None] * value
                obuf[:, tt, level, rows, :] = value

    def settle(c):
        tt = c // halves
        base = (c % halves) * rows_of
        reach = []
        for r in ratios(me * mine + tt):
            step = r / (1.0 + r)
            reach.append(reach[-1] * step if reach else step)

        def add_above(level):
            @pl.loop(0, rows_of // SUB)
            def _(g):
                rows = pl.ds(pl.multiple_of(base + g * SUB, SUB), SUB)
                obuf[:, tt, level, rows, :] += reach[level][None] * zin[:, tt, rows, :]

        @pl.when(lev > 0)
        def _():
            downward(c).wait_recv()
            add_above(levels - 1)

        @pl.when(lev < depth - 1)
        def _():
            downward(c).start()

        @pl.when(lev > 0)
        def _():
            for level in range(levels - 1):
                add_above(level)

    def send_home(tt):
        @pl.loop(1, n)
        def _(k):
            homeward(tt, k).start()

        own_out(tt).start()

    hold = min(HOLD, count - 1)

    @pl.loop(0, count + depth - 1)
    def _(i):
        @pl.when(i < count)
        def _():
            turn(i)

        done = i - lev

        @pl.when((done >= 0) & (done < count))
        def _():
            settle(done)

        @pl.when((done >= 0) & (done < count) & (done % halves == halves - 1) & (i > hold))
        def _():
            send_home(done // halves)

        @pl.when(i == hold)
        def _():
            @pl.loop(0, mine)
            def _(tt):
                @pl.when((tt + 1) * halves - 1 <= done)
                def _():
                    send_home(tt)

    @pl.when(lev < depth - 1)
    def _():
        @pl.loop(0, count)
        def _(c):
            downward(c).wait_send()

    @pl.loop(0, mine)
    def _(tt):
        own_out(tt).wait()

        @pl.loop(1, n)
        def _(k):
            outward(tt, k).wait_send()
            homeward(tt, k).wait()


def by_tracer(tracers, offsets, fraction, bin_class, thickness):
    count, levels, lats, width = tracers.shape
    n = lax.axis_size("lon")
    depth = lax.axis_size("lev")
    mine = count // n
    pieces = mine * max(1, min(PIECES // mine, lats // SUB))
    hbm = pl.BlockSpec(memory_space=pltpu.HBM)
    held = [pltpu.SMEM(a.shape, a.dtype) for a in (offsets, fraction, bin_class, thickness)]
    sem = pltpu.SemaphoreType.DMA
    return pl.pallas_call(
        functools.partial(exchange_kernel, n, depth),
        out_shape=jax.ShapeDtypeStruct(tracers.shape, jnp.float32),
        in_specs=[hbm] * 5,
        out_specs=pl.BlockSpec(memory_space=pl.ANY),
        scratch_shapes=[
            *held, sem((4,)),
            pltpu.VMEM((n, mine, levels, lats, width), jnp.float32),
            pltpu.VMEM((n, mine, levels, lats, width), jnp.float32),
            pltpu.VMEM((n, mine, lats, width), jnp.float32),
            pltpu.VMEM((lats, width), jnp.int32),
            pltpu.VMEM((lats, width), jnp.float32),
            sem((mine, n)), sem((mine, n)), sem((mine, n)), sem((mine, n)),
            sem((mine,)), sem((mine,)), sem((pieces,)), sem((pieces,)),
        ],
        compiler_params=pltpu.CompilerParams(
            collective_id=0, has_side_effects=True, vmem_limit_bytes=24 << 20),
    )(*(pltpu.with_memory_space_constraint(a, pltpu.HBM)
        for a in (tracers, offsets, fraction, bin_class, thickness)))


def plan_kernel(chips, tiers, lats, offsets_ref, table_ref, tier_ref, column):
    pieces, width = column.shape
    entry_rows = (table_ref.shape[0] - 3) // SEGMENTS

    @pl.loop(0, pieces, unroll=8)
    def _(i):
        column[pl.ds(i, 1), :] = jnp.full((1, width), offsets_ref[lax.rem(i, lats)], jnp.int32)

    shift = column[...]
    lane = lax.broadcasted_iota(jnp.int32, shift.shape, 1)
    row = lax.broadcasted_iota(jnp.int32, shift.shape, 0)

    def total(value, axis):
        return jnp.sum(value.astype(jnp.float32), axis=axis, keepdims=True).astype(jnp.int32)

    def flat(value):
        return total(jnp.where(lane == row, value, 0), 0)

    def count(chosen, axis):
        return total(jnp.where(chosen, 1.0, 0.0), axis)

    def onward(chip, by):
        moved = chip + by
        return jnp.where(moved >= chips, moved - chips, moved)

    block = lax.div(shift, width)
    rest = lax.rem(shift, width)
    chip, odd = lax.div(block, 2), lax.rem(block, 2)
    lower = row >= lats
    lat = jnp.where(lower, row - lats, row)
    away = jnp.where(lower, onward(chip, 1), chip)
    size = jnp.where(lower, rest + 1, width - rest)
    start = width - size
    start = jnp.where(lower, start, 0)
    source = 2 * lat + 1 - odd
    whole = jnp.where(lower, -1, onward(chip, odd))
    whole_source = 2 * lat + odd

    whole_of = flat(whole + 1) - 1
    place = count((whole_of == whole) & (lane < row), 1)
    away_of, size_of = flat(away), flat(size)
    same = away_of == away
    rank = count(same & ((size_of < size) | ((size_of == size) & (lane < row))), 1)
    number = count(same, 1)
    order = jnp.where(rank < lax.div(number, 2), 2 * rank + 1, 2 * (number - 1 - rank))
    before = same & (flat(order + jnp.zeros_like(shift)) < order)
    turn = count(before, 1)
    position = total(jnp.where(before, size_of, 0), 1)

    wholes, need = [], 0
    for d in range(chips):
        wholes.append(count(whole == d, 0))
        cells = total(jnp.where(away == d, size, 0), 0)
        if d:
            need = jnp.maximum(need, wholes[d] + lax.div(cells + width - 1, width))
    slots, tier = tiers[0], 0
    for smaller, larger in zip(tiers, tiers[1:] + tiers[-1:]):
        slots = jnp.where(need > smaller, larger, slots)
        tier = tier + jnp.where(need > smaller, 1, 0)

    skip = 0
    for d in range(chips):
        skip = skip + jnp.where(away == d, wholes[d], 0)
    own = 2 * lats
    here = away == 0
    first_entry = (away - 1) * slots + skip + lax.div(position, width)
    offset = jnp.where(here, start, lax.rem(position, width))
    whole_entry = jnp.where(whole <= 0, -1, (whole - 1) * slots + place)
    pool = jnp.where(here, source, own + first_entry)
    back = rest + start - offset
    back = jnp.where(back < 0, back + width, back)
    back = jnp.where(back >= width, back - width, back)
    table_ref[pl.ds(0, 1), :] = flat(jnp.where(whole == 0, whole_source, own + whole_entry))
    table_ref[pl.ds(1, 1), :] = flat(pool + (offset << 9) + (back << 16))
    table_ref[pl.ds(2, 1), :] = flat(rest)

    forth = offset - start
    forth = jnp.where(forth < 0, forth + width, forth)
    word = source + (forth << 7)
    deepest = jnp.zeros((1, width), jnp.float32)
    for w in range(entry_rows):
        entry = lane + w * width
        begin = jnp.where(here, -4 * width, (first_entry - entry) * width + offset)
        end = begin + size
        touches = (begin < width) & (end > 0)
        earliest = jnp.min(jnp.where(touches, turn, pieces).astype(jnp.float32), axis=0, keepdims=True).astype(jnp.int32)
        segment = jnp.where(touches, turn - earliest, -1)
        deepest = jnp.maximum(deepest, jnp.max(segment.astype(jnp.float32), axis=0, keepdims=True))
        bounded = word + (jnp.minimum(end, width) << 14)
        for k in range(SEGMENTS):
            value = jnp.where(segment == k, bounded, 0)
            if k == 0:
                value += jnp.where(whole_entry == entry, whole_source + (width << 14), 0)
            table_ref[pl.ds(3 + k * entry_rows + w, 1), :] = total(value, 0)
    tier = jnp.where(deepest >= SEGMENTS, len(tiers), tier)
    tier_ref[0] = jnp.max(tier.astype(jnp.float32)).astype(jnp.int32)


def chunks_of(groups):
    sizes = [1] * groups if groups < 6 else [1, 1] + [2] * ((groups - 4) // 2) + [1] * (groups % 2 + 2)
    return [(sum(sizes[:c]), size) for c, size in enumerate(sizes)]


def direct_kernel(
    n, depth, slots, lats, levels, x_ref, table_hbm, fraction_hbm, class_hbm, thick_hbm, out_ref,
    table_ref, fraction_ref, class_ref, thick_ref, small, xin, xe, outb, zin, zout,
    own1, xs, xr, ss, rs, zs, zr, own2, hs, hr, *buffers,
):
    _, groups, _, width = xin.shape
    chips = n // 2
    own = 2 * lats
    entry_rows = (table_ref.shape[0] - 3) // SEGMENTS
    each = SUB // levels
    parts = chunks_of(groups)
    chunks = len(parts)
    sends, pools = buffers[:chunks], buffers[chunks:]
    late = chunks // 2
    me = lax.axis_index("lon")
    lev = lax.axis_index("lev")
    core = lax.rem(me, 2)
    partner = me + 1 - 2 * core

    def peer(d):
        return lax.rem(me + 2 * d, n)

    def part(c, side):
        first, size = parts[c]
        return pl.ds(side * groups + first, size)

    def local(c):
        first, size = parts[c]
        return pl.ds(first, size)

    def own_in(c):
        return pltpu.make_async_copy(x_ref.at[part(c, core)], xin.at[core, local(c)], own1.at[c])

    def swap_in(c):
        return pltpu.make_async_remote_copy(
            src_ref=x_ref.at[part(c, 1 - core)], dst_ref=xin.at[core, local(c)],
            send_sem=xs.at[c], recv_sem=xr.at[c],
            device_id={"lon": partner}, device_id_type=pl.DeviceIdType.MESH,
        )

    def onward(c, d):
        return pltpu.make_async_remote_copy(
            src_ref=sends[c].at[pl.ds((d - 1) * slots, slots)],
            dst_ref=pools[c].at[pl.ds(own + (d - 1) * slots, slots)],
            send_sem=ss.at[c, d], recv_sem=rs.at[c, d],
            device_id={"lon": peer(d)}, device_id_type=pl.DeviceIdType.MESH,
        )

    def downward(g):
        return pltpu.make_async_remote_copy(
            src_ref=zout.at[g], dst_ref=zin.at[g], send_sem=zs.at[g], recv_sem=zr.at[g],
            device_id={"lev": lax.rem(lev + 1, depth)}, device_id_type=pl.DeviceIdType.MESH,
        )

    def own_out(c):
        return pltpu.make_async_copy(outb.at[core, local(c)], out_ref.at[part(c, core)], own2.at[c])

    def swap_out(c):
        return pltpu.make_async_remote_copy(
            src_ref=outb.at[1 - core, local(c)], dst_ref=out_ref.at[part(c, core)],
            send_sem=hs.at[c], recv_sem=hr.at[c],
            device_id={"lon": partner}, device_id_type=pl.DeviceIdType.MESH,
        )

    scalars = [
        pltpu.make_async_copy(source, held, small.at[i])
        for i, (source, held) in enumerate((
            (table_hbm, table_ref), (fraction_hbm, fraction_ref),
            (class_hbm, class_ref), (thick_hbm, thick_ref)))
    ]
    barrier = pltpu.get_barrier_semaphore()
    pl.semaphore_signal(barrier, inc=1, device_id={"lon": partner}, device_id_type=pl.DeviceIdType.MESH)
    for d in range(1, chips):
        pl.semaphore_signal(barrier, inc=1, device_id={"lon": peer(d)}, device_id_type=pl.DeviceIdType.MESH)
    for k in (1, depth - 1):
        pl.semaphore_signal(barrier, inc=1, device_id={"lev": lax.rem(lev + k, depth)},
                            device_id_type=pl.DeviceIdType.MESH)
    for c in range(chunks):
        own_in(c).start()
    for copy in scalars:
        copy.start()
    pl.semaphore_wait(barrier, chips + 2)
    for c in range(chunks):
        swap_in(c).start()
    for copy in scalars:
        copy.wait()

    def ratios(tracer):
        bin_class = jnp.full((SUB, width), class_ref[tracer // GROUPS], jnp.int32)
        speed = 0.5
        for b in range(3):
            speed = speed * jnp.where((bin_class & (1 << b)) != 0, 2.0 ** (1 << b), 1.0)
        return [speed / thick_ref[level] for level in range(levels)]

    def rolls(value, by):
        return pltpu.roll(value, by, axis=1)

    def spread(c):
        first, size = parts[c]

        @pl.loop(0, lats, unroll=8 // size)
        def _(j):
            for side in (0, 1):
                for g in range(size):
                    value = xin[side, first + g, pl.ds(j, SUB, stride=lats), :]
                    at = pl.ds(g * SUB, SUB)
                    xe[2 * j + side, at] = value
                    pools[c][2 * j + side, at] = value

    def pack(c):
        size = parts[c][1]
        lane = lax.broadcasted_iota(jnp.int32, (size * SUB, width), 1)
        unroll = 8 // size
        rounded = -(-slots // unroll) * unroll

        @pl.loop(1, chips)
        def _(d):
            @pl.loop(0, rounded, unroll=unroll)
            def _(i):
                e = (d - 1) * slots + i
                value = None
                for k in reversed(range(SEGMENTS)):
                    word = table_ref[3 + k * entry_rows + lax.div(e, width), lax.rem(e, width)]
                    piece = rolls(xe[word & (own - 1), pl.ds(0, size * SUB)], (word >> 7) & (width - 1))
                    value = piece if value is None else jnp.where(lane < (word >> 14), piece, value)
                sends[c][e] = value

            onward(c, d).start()

    def unpack(c):
        first, size = parts[c]
        pool = pools[c]
        lane = lax.broadcasted_iota(jnp.int32, (size * SUB, width), 1)
        edge = lane == 0

        def piece(word):
            at = word & 511
            both = jnp.where(lane >= ((word >> 9) & (width - 1)), pool[at], pool[at + 1])
            return rolls(both, word >> 16)

        @pl.loop(0, lats, unroll=16 // size)
        def _(j):
            share = fraction_ref[j]
            rest = table_ref[2, j]
            full = rolls(pool[table_ref[0, j]], rest)
            high = piece(table_ref[1, j])
            low = piece(table_ref[1, lats + j])
            left = jnp.where(lane < rest, low, full)
            right = jnp.where(lane < rest, full, high)
            left_turned = rolls(left, 1)
            left_before = jnp.where(edge, rolls(low, 1), left_turned)
            right_before = jnp.where(edge, left_turned, rolls(right, 1))
            left = (1.0 - share) * left + share * left_before
            right = (1.0 - share) * right + share * right_before
            for g in range(size):
                outb[0, first + g, pl.ds(j, SUB, stride=lats), :] = left[g * SUB:(g + 1) * SUB]
                outb[1, first + g, pl.ds(j, SUB, stride=lats), :] = right[g * SUB:(g + 1) * SUB]

    def rows(tt, level, i):
        return pl.ds(pl.multiple_of((tt * levels + level) * lats + i * SUB, SUB), SUB)

    def bottom(side, tt, i):
        return pl.ds(pl.multiple_of((side * each + tt) * lats + i * SUB, SUB), SUB)

    def settle(held, c):
        @pl.loop(parts[c][0], sum(parts[c]))
        def _(g):
            for tt in range(each):
                ratio = ratios((core * groups + g) * each + tt)
                keep = [1.0 / (1.0 + r) for r in ratio]
                carry = [r * k for r, k in zip(ratio, keep)]

                @pl.loop(0, lats // SUB, unroll=2)
                def _(i):
                    for side in (0, 1):
                        value = None
                        for level in range(levels):
                            field = keep[level] * held[side, g, rows(tt, level, i), :]
                            value = field if value is None else field + carry[level] * value
                            held[side, g, rows(tt, level, i), :] = value
                        zout[g, bottom(side, tt, i), :] = value

            @pl.when((lev == 0) & (depth > 1))
            def _():
                downward(g).start()

    def sink(held, c):
        def reach_of(g, tt):
            reach = []
            for r in ratios((core * groups + g) * each + tt):
                step = r / (1.0 + r)
                reach.append(reach[-1] * step if reach else step)
            return reach

        @pl.when(lev > 0)
        def _():
            @pl.loop(parts[c][0], sum(parts[c]))
            def _(g):
                downward(g).wait_recv()
                for tt in range(each):
                    last = reach_of(g, tt)[-1]

                    @pl.loop(0, lats // SUB, unroll=2)
                    def _(i):
                        for side in (0, 1):
                            at = bottom(side, tt, i)
                            value = zout[g, at, :] + last * zin[g, at, :]
                            zout[g, at, :] = value
                            held[side, g, rows(tt, levels - 1, i), :] = value

                @pl.when(lev < depth - 1)
                def _():
                    downward(g).start()

        @pl.when(lev > 0)
        def _():
            @pl.loop(parts[c][0], sum(parts[c]))
            def _(g):
                for tt in range(each):
                    reach = reach_of(g, tt)

                    @pl.loop(0, lats // SUB, unroll=2)
                    def _(i):
                        for side in (0, 1):
                            above = zin[g, bottom(side, tt, i), :]
                            for level in range(levels - 1):
                                held[side, g, rows(tt, level, i), :] += reach[level] * above

    def arrive(c):
        own_in(c).wait()
        swap_in(c).wait_recv()

    for c in range(late):
        arrive(c)
        spread(c)
        pack(c)
        if c == 0:
            for later in range(late, chunks):
                arrive(later)
                settle(xin, later)
    for c in range(late, chunks):
        sink(xin, c)
        spread(c)
        pack(c)
    for c in range(chunks):
        @pl.loop(1, chips)
        def _(d):
            onward(c, d).wait_recv()

        unpack(c)
        if c < late:
            settle(outb, c)
            sink(outb, c)
        own_out(c).start()
        swap_out(c).start()

    @pl.when(lev < depth - 1)
    def _():
        @pl.loop(0, groups)
        def _(g):
            downward(g).wait_send()

    for c in range(chunks):
        swap_in(c).wait_send()

        @pl.loop(1, chips)
        def _(d):
            onward(c, d).wait_send()

        own_out(c).wait()
        swap_out(c).wait()


def in_hbm(arrays):
    return tuple(pltpu.with_memory_space_constraint(a, pltpu.HBM) for a in arrays)


def make_plan(offsets, chips, width, tiers):
    lats = offsets.shape[0]
    words = -(-(chips - 1) * tiers[-1] // width)
    return pl.pallas_call(
        functools.partial(plan_kernel, chips, tiers, lats),
        out_shape=(jax.ShapeDtypeStruct((3 + SEGMENTS * words, width), jnp.int32), jax.ShapeDtypeStruct((1,), jnp.int32)),
        in_specs=[pl.BlockSpec(memory_space=pltpu.SMEM)],
        out_specs=(pl.BlockSpec(memory_space=pltpu.VMEM), pl.BlockSpec(memory_space=pltpu.SMEM)),
        scratch_shapes=[pltpu.VMEM((2 * lats, width), jnp.int32)],
    )(offsets)


def direct(slots, identity, tracers, table, fraction, bin_class, thickness):
    count, levels, lats, width = tracers.shape
    n = lax.axis_size("lon")
    depth = lax.axis_size("lev")
    chips = n // 2
    groups = count * levels // (2 * SUB)
    chunks = chunks_of(groups)
    span = SUB * lats
    entries = (chips - 1) * slots
    hbm = pl.BlockSpec(memory_space=pltpu.HBM)
    held = [pltpu.SMEM(a.shape, a.dtype) for a in (table, fraction, bin_class, thickness)]
    sem = pltpu.SemaphoreType.DMA
    many = sem((len(chunks),))
    edge = 2 * (SUB // levels) * lats

    def vmem(*shape):
        return pltpu.VMEM((*shape, width), jnp.float32)

    out = pl.pallas_call(
        functools.partial(direct_kernel, n, depth, slots, lats, levels),
        out_shape=jax.ShapeDtypeStruct((2 * groups, span, width), jnp.float32),
        in_specs=[hbm] * 5,
        out_specs=pl.BlockSpec(memory_space=pl.ANY),
        scratch_shapes=[
            *held, sem((4,)),
            vmem(2, groups, span), vmem(2 * lats, 2 * SUB), vmem(2, groups, span),
            vmem(groups, edge), vmem(groups, edge),
            many, many, many, sem((len(chunks), chips)), sem((len(chunks), chips)),
            sem((groups,)), sem((groups,)), many, many, many,
            *[vmem(entries + 8, size * SUB) for _, size in chunks],
            *[vmem(2 * lats + entries + 1, size * SUB) for _, size in chunks],
        ],
        compiler_params=pltpu.CompilerParams(
            collective_id=identity, has_side_effects=True, vmem_limit_bytes=44 << 20),
    )(*in_hbm((tracers.reshape(2 * groups, span, width), table, fraction, bin_class, thickness)))
    return out.reshape(tracers.shape)


def on_device(tracers, offsets, fraction, bin_class, thickness):
    count, levels, lats, width = tracers.shape
    n = lax.axis_size("lon")
    if width != 128 or lats != 64 or n % 2 or n < 4 or SUB % levels or count * levels % (2 * SUB):
        return by_tracer(tracers, offsets, fraction, bin_class, thickness)
    tiers = []
    for share in SHARES:
        slots = -(-share * lats // (16 * (n // 2)))
        slots += slots % 2
        if slots not in tiers:
            tiers.append(slots)
    table, tier = make_plan(offsets, n // 2, width, tiers)
    ways = [
        functools.partial(lambda slots, i, x, o, t, f, b, h: direct(slots, i, x, t, f, b, h), slots, i + 1)
        for i, slots in enumerate(tiers)
    ]
    ways.append(lambda x, o, t, f, b, h: by_tracer(x, o, f, b, h))
    return lax.switch(tier[0], ways, tracers, offsets, table, fraction, bin_class, thickness)


def solution(mesh):
    in_specs = (P(None, "lev", None, "lon"), P(), P(), P(), P("lev"))
    out_specs = P(None, "lev", None, "lon")
    return jax.shard_map(
        on_device, mesh=mesh, in_specs=in_specs, out_specs=out_specs, check_vma=False
    )
```

```python
import functools

import jax
import jax.numpy as jnp
from jax import lax
from jax.experimental import pallas as pl
from jax.experimental.pallas import tpu as pltpu
from jax.sharding import PartitionSpec as P

GROUPS = 4
SUB = 8
PIECES = 8
HOLD = 3
SHARES = (32, 34, 36, 38, 40, 44, 50)
SEGMENTS = 5


def exchange_kernel(
    n, depth, x_ref, offsets_hbm, fraction_hbm, class_hbm, thick_hbm, out_ref,
    offsets_ref, fraction_ref, class_ref, thick_ref, small, recv, obuf, zin, row_ref, share_ref, s1, r1, s2, r2, own1, own2, zs, zr,
):
    tracers, levels, lats, width = x_ref.shape
    mine = tracers // n
    halves = max(1, min(PIECES // mine, lats // SUB))
    rows_of = lats // halves
    me = lax.axis_index("lon")
    lev = lax.axis_index("lev")

    def at(c):
        return c // halves, pl.ds(pl.multiple_of((c % halves) * rows_of, SUB), rows_of)

    def peer(k):
        return lax.rem(me + k, n)

    def outward(tt, k):
        return pltpu.make_async_remote_copy(
            src_ref=x_ref.at[peer(k) * mine + tt],
            dst_ref=recv.at[me, tt],
            send_sem=s1.at[tt, k], recv_sem=r1.at[tt, k],
            device_id={"lon": peer(k)}, device_id_type=pl.DeviceIdType.MESH,
        )

    def homeward(tt, k):
        return pltpu.make_async_remote_copy(
            src_ref=obuf.at[peer(k), tt],
            dst_ref=out_ref.at[me * mine + tt],
            send_sem=s2.at[tt, k], recv_sem=r2.at[tt, k],
            device_id={"lon": peer(k)}, device_id_type=pl.DeviceIdType.MESH,
        )

    def downward(c):
        tt, rows = at(c)
        return pltpu.make_async_remote_copy(
            src_ref=obuf.at[:, tt, levels - 1, rows, :],
            dst_ref=zin.at[:, tt, rows, :],
            send_sem=zs.at[c], recv_sem=zr.at[c],
            device_id={"lev": lax.rem(lev + 1, depth)}, device_id_type=pl.DeviceIdType.MESH,
        )

    def own_in(tt):
        return pltpu.make_async_copy(x_ref.at[me * mine + tt], recv.at[me, tt], own1.at[tt])

    def own_out(tt):
        return pltpu.make_async_copy(obuf.at[me, tt], out_ref.at[me * mine + tt], own2.at[tt])

    scalars = [
        pltpu.make_async_copy(source, held, small.at[i])
        for i, (source, held) in enumerate((
            (offsets_hbm, offsets_ref), (fraction_hbm, fraction_ref),
            (class_hbm, class_ref), (thick_hbm, thick_ref)))
    ]
    for copy in scalars:
        copy.start()

    barrier = pltpu.get_barrier_semaphore()
    for k in range(1, n):
        pl.semaphore_signal(barrier, inc=1, device_id={"lon": peer(k)},
                            device_id_type=pl.DeviceIdType.MESH)
    for k in (1, depth - 1):
        pl.semaphore_signal(barrier, inc=1, device_id={"lev": lax.rem(lev + k, depth)},
                            device_id_type=pl.DeviceIdType.MESH)
    pl.semaphore_wait(barrier, n + 1)

    count = mine * halves

    @pl.loop(0, mine)
    def _(tt):
        @pl.loop(1, n)
        def _(k):
            outward(tt, k).start()

        own_in(tt).start()

    for copy in scalars:
        copy.wait()

    @pl.loop(0, lats)
    def _(j):
        shift = jnp.full((1, width), offsets_ref[j], jnp.int32)
        row_ref[pl.ds(j, 1), :] = shift
        share_ref[pl.ds(j, 1), :] = jnp.full((1, width), fraction_ref[j], jnp.float32)

    def ratios(tracer):
        bin_class = jnp.full((SUB, width), class_ref[tracer // GROUPS], jnp.int32)
        speed = 0.5
        for b in range(3):
            speed = speed * jnp.where((bin_class & (1 << b)) != 0, 2.0 ** (1 << b), 1.0)
        return [speed / thick_ref[level] for level in range(levels)]

    lane = lax.broadcasted_iota(jnp.int32, (SUB, width), 1)

    def behind(value, by):
        by %= n
        if by == 0:
            return value
        return jnp.concatenate([value[n - by:], value[:n - by]], axis=0)

    def turn(c):
        tt = c // halves
        base = (c % halves) * rows_of
        ratio = ratios(me * mine + tt)
        keep = [1.0 / (1.0 + r) for r in ratio]
        carry = [r * k for r, k in zip(ratio, keep)]

        @pl.when(c % halves == 0)
        def _():
            own_in(tt).wait()

            @pl.loop(1, n)
            def _(k):
                outward(tt, k).wait_recv()

        @pl.loop(0, rows_of // SUB)
        def _(g):
            rows = pl.ds(pl.multiple_of(base + g * SUB, SUB), SUB)
            shift = row_ref[rows, :]
            remainder = lax.rem(shift, width)
            quotient = lax.div(shift, width)
            share = share_ref[rows, :]
            fine = [(remainder & (1 << b)) != 0 for b in range((width - 1).bit_length())]
            coarse = [(quotient & (1 << b)) != 0 for b in range((n - 1).bit_length())]
            same_block = lane >= remainder
            first_lane = lane == 0
            value = None
            for level in range(levels):
                field = recv[:, tt, level, rows, :]
                turned = pltpu.roll(field, 1, axis=2)
                left = jnp.where(first_lane[None], behind(turned, 1), turned)
                field = (1.0 - share)[None] * field + share[None] * left
                for b, chosen in enumerate(fine):
                    field = jnp.where(chosen[None], pltpu.roll(field, 1 << b, axis=2), field)
                field = jnp.where(same_block[None], field, behind(field, 1))
                for b, chosen in enumerate(coarse):
                    field = jnp.where(chosen[None], behind(field, 1 << b), field)
                field = keep[level][None] * field
                value = field if value is None else field + carry[level][None] * value
                obuf[:, tt, level, rows, :] = value

    def settle(c):
        tt = c // halves
        base = (c % halves) * rows_of
        reach = []
        for r in ratios(me * mine + tt):
            step = r / (1.0 + r)
            reach.append(reach[-1] * step if reach else step)

        def add_above(level):
            @pl.loop(0, rows_of // SUB)
            def _(g):
                rows = pl.ds(pl.multiple_of(base + g * SUB, SUB), SUB)
                obuf[:, tt, level, rows, :] += reach[level][None] * zin[:, tt, rows, :]

        @pl.when(lev > 0)
        def _():
            downward(c).wait_recv()
            add_above(levels - 1)

        @pl.when(lev < depth - 1)
        def _():
            downward(c).start()

        @pl.when(lev > 0)
        def _():
            for level in range(levels - 1):
                add_above(level)

    def send_home(tt):
        @pl.loop(1, n)
        def _(k):
            homeward(tt, k).start()

        own_out(tt).start()

    hold = min(HOLD, count - 1)

    @pl.loop(0, count + depth - 1)
    def _(i):
        @pl.when(i < count)
        def _():
            turn(i)

        done = i - lev

        @pl.when((done >= 0) & (done < count))
        def _():
            settle(done)

        @pl.when((done >= 0) & (done < count) & (done % halves == halves - 1) & (i > hold))
        def _():
            send_home(done // halves)

        @pl.when(i == hold)
        def _():
            @pl.loop(0, mine)
            def _(tt):
                @pl.when((tt + 1) * halves - 1 <= done)
                def _():
                    send_home(tt)

    @pl.when(lev < depth - 1)
    def _():
        @pl.loop(0, count)
        def _(c):
            downward(c).wait_send()

    @pl.loop(0, mine)
    def _(tt):
        own_out(tt).wait()

        @pl.loop(1, n)
        def _(k):
            outward(tt, k).wait_send()
            homeward(tt, k).wait()


def by_tracer(tracers, offsets, fraction, bin_class, thickness):
    count, levels, lats, width = tracers.shape
    n = lax.axis_size("lon")
    depth = lax.axis_size("lev")
    mine = count // n
    pieces = mine * max(1, min(PIECES // mine, lats // SUB))
    hbm = pl.BlockSpec(memory_space=pltpu.HBM)
    held = [pltpu.SMEM(a.shape, a.dtype) for a in (offsets, fraction, bin_class, thickness)]
    sem = pltpu.SemaphoreType.DMA
    return pl.pallas_call(
        functools.partial(exchange_kernel, n, depth),
        out_shape=jax.ShapeDtypeStruct(tracers.shape, jnp.float32),
        in_specs=[hbm] * 5,
        out_specs=pl.BlockSpec(memory_space=pl.ANY),
        scratch_shapes=[
            *held, sem((4,)),
            pltpu.VMEM((n, mine, levels, lats, width), jnp.float32),
            pltpu.VMEM((n, mine, levels, lats, width), jnp.float32),
            pltpu.VMEM((n, mine, lats, width), jnp.float32),
            pltpu.VMEM((lats, width), jnp.int32),
            pltpu.VMEM((lats, width), jnp.float32),
            sem((mine, n)), sem((mine, n)), sem((mine, n)), sem((mine, n)),
            sem((mine,)), sem((mine,)), sem((pieces,)), sem((pieces,)),
        ],
        compiler_params=pltpu.CompilerParams(
            collective_id=0, has_side_effects=True, vmem_limit_bytes=24 << 20),
    )(*(pltpu.with_memory_space_constraint(a, pltpu.HBM)
        for a in (tracers, offsets, fraction, bin_class, thickness)))


def plan_kernel(
    chips, tiers, lats, groups, offsets_ref, x_ref, table_ref, tier_ref, head_ref, column, own_sem, send_sem, recv_sem,
):
    pieces, width = column.shape
    entry_rows = (table_ref.shape[0] - 3) // SEGMENTS
    me = lax.axis_index("lon")
    core = lax.rem(me, 2)
    partner = {"lon": me + 1 - 2 * core}
    barrier = pltpu.get_barrier_semaphore()
    pl.semaphore_signal(barrier, inc=1, device_id=partner, device_id_type=pl.DeviceIdType.MESH)
    keep = pltpu.make_async_copy(x_ref.at[pl.ds(core * groups, 1)], head_ref.at[core], own_sem)
    give = pltpu.make_async_remote_copy(
        src_ref=x_ref.at[pl.ds((1 - core) * groups, 1)], dst_ref=head_ref.at[core],
        send_sem=send_sem, recv_sem=recv_sem,
        device_id=partner, device_id_type=pl.DeviceIdType.MESH,
    )
    keep.start()

    @pl.loop(0, pieces, unroll=8)
    def _(i):
        column[pl.ds(i, 1), :] = jnp.full((1, width), offsets_ref[lax.rem(i, lats)], jnp.int32)

    pl.semaphore_wait(barrier, 1)
    give.start()
    shift = column[...]
    lane = lax.broadcasted_iota(jnp.int32, shift.shape, 1)
    row = lax.broadcasted_iota(jnp.int32, shift.shape, 0)

    def total(value, axis):
        return jnp.sum(value.astype(jnp.float32), axis=axis, keepdims=True).astype(jnp.int32)

    def flat(value):
        return total(jnp.where(lane == row, value, 0), 0)

    def count(chosen, axis):
        return total(jnp.where(chosen, 1.0, 0.0), axis)

    def onward(chip, by):
        moved = chip + by
        return jnp.where(moved >= chips, moved - chips, moved)

    block = lax.div(shift, width)
    rest = lax.rem(shift, width)
    chip, odd = lax.div(block, 2), lax.rem(block, 2)
    lower = row >= lats
    lat = jnp.where(lower, row - lats, row)
    away = jnp.where(lower, onward(chip, 1), chip)
    size = jnp.where(lower, rest + 1, width - rest)
    start = width - size
    start = jnp.where(lower, start, 0)
    source = 2 * lat + 1 - odd
    whole = jnp.where(lower, -1, onward(chip, odd))
    whole_source = 2 * lat + odd

    whole_of = flat(whole + 1) - 1
    place = count((whole_of == whole) & (lane < row), 1)
    away_of, size_of = flat(away), flat(size)
    same = away_of == away
    rank = count(same & ((size_of < size) | ((size_of == size) & (lane < row))), 1)
    number = count(same, 1)
    order = jnp.where(rank < lax.div(number, 2), 2 * rank + 1, 2 * (number - 1 - rank))
    before = same & (flat(order + jnp.zeros_like(shift)) < order)
    turn = count(before, 1)
    position = total(jnp.where(before, size_of, 0), 1)

    wholes, need = [], 0
    for d in range(chips):
        wholes.append(count(whole == d, 0))
        cells = total(jnp.where(away == d, size, 0), 0)
        if d:
            need = jnp.maximum(need, wholes[d] + lax.div(cells + width - 1, width))
    slots, tier = tiers[0], 0
    for smaller, larger in zip(tiers, tiers[1:] + tiers[-1:]):
        slots = jnp.where(need > smaller, larger, slots)
        tier = tier + jnp.where(need > smaller, 1, 0)

    skip = 0
    for d in range(chips):
        skip = skip + jnp.where(away == d, wholes[d], 0)
    own = 2 * lats
    here = away == 0
    first_entry = (away - 1) * slots + skip + lax.div(position, width)
    offset = jnp.where(here, start, lax.rem(position, width))
    whole_entry = jnp.where(whole <= 0, -1, (whole - 1) * slots + place)
    pool = jnp.where(here, source, own + first_entry)
    back = rest + start - offset
    back = jnp.where(back < 0, back + width, back)
    back = jnp.where(back >= width, back - width, back)
    table_ref[pl.ds(0, 1), :] = flat(jnp.where(whole == 0, whole_source, own + whole_entry))
    table_ref[pl.ds(1, 1), :] = flat(pool + (offset << 9) + (back << 16))
    table_ref[pl.ds(2, 1), :] = flat(rest)

    forth = offset - start
    forth = jnp.where(forth < 0, forth + width, forth)
    word = source + (forth << 7)
    deepest = jnp.zeros((1, width), jnp.float32)
    for w in range(entry_rows):
        entry = lane + w * width
        begin = jnp.where(here, -4 * width, (first_entry - entry) * width + offset)
        end = begin + size
        touches = (begin < width) & (end > 0)
        earliest = jnp.min(jnp.where(touches, turn, pieces).astype(jnp.float32), axis=0, keepdims=True).astype(jnp.int32)
        segment = jnp.where(touches, turn - earliest, -1)
        deepest = jnp.maximum(deepest, jnp.max(segment.astype(jnp.float32), axis=0, keepdims=True))
        bounded = word + (jnp.minimum(end, width) << 14)
        for k in range(SEGMENTS):
            value = jnp.where(segment == k, bounded, 0)
            if k == 0:
                value += jnp.where(whole_entry == entry, whole_source + (width << 14), 0)
            table_ref[pl.ds(3 + k * entry_rows + w, 1), :] = total(value, 0)
    tier = jnp.where(deepest >= SEGMENTS, len(tiers), tier)
    tier_ref[0] = jnp.max(tier.astype(jnp.float32)).astype(jnp.int32)
    keep.wait()
    give.wait()


def chunks_of(groups):
    sizes = [1] * groups if groups < 4 else [1] + [2] * ((groups - 2) // 2) + [1] * (groups % 2 + 1)
    return [(sum(sizes[:c]), size) for c, size in enumerate(sizes)]


def direct_kernel(
    n, depth, slots, lats, levels, x_ref, head_ref, table_hbm, fraction_hbm, class_hbm, thick_hbm, out_ref,
    table_ref, fraction_ref, class_ref, thick_ref, small, xin, xe, outb, zin, zout,
    own1, xs, xr, ss, rs, zs, zr, own2, hs, hr, *buffers,
):
    _, groups, _, width = xin.shape
    chips = n // 2
    own = 2 * lats
    entry_rows = (table_ref.shape[0] - 3) // SEGMENTS
    each = SUB // levels
    parts = chunks_of(groups)
    chunks = len(parts)
    sends, pools = buffers[:chunks], buffers[chunks:]
    late = chunks // 2
    me = lax.axis_index("lon")
    lev = lax.axis_index("lev")
    core = lax.rem(me, 2)
    partner = me + 1 - 2 * core

    def peer(d):
        return lax.rem(me + 2 * d, n)

    def part(c, side):
        first, size = parts[c]
        return pl.ds(side * groups + first, size)

    def local(c):
        first, size = parts[c]
        return pl.ds(first, size)

    def own_in(c):
        return pltpu.make_async_copy(x_ref.at[part(c, core)], xin.at[core, local(c)], own1.at[c])

    def swap_in(c):
        return pltpu.make_async_remote_copy(
            src_ref=x_ref.at[part(c, 1 - core)], dst_ref=xin.at[core, local(c)],
            send_sem=xs.at[c], recv_sem=xr.at[c],
            device_id={"lon": partner}, device_id_type=pl.DeviceIdType.MESH,
        )

    def onward(c, d):
        return pltpu.make_async_remote_copy(
            src_ref=sends[c].at[pl.ds((d - 1) * slots, slots)],
            dst_ref=pools[c].at[pl.ds(own + (d - 1) * slots, slots)],
            send_sem=ss.at[c, d], recv_sem=rs.at[c, d],
            device_id={"lon": peer(d)}, device_id_type=pl.DeviceIdType.MESH,
        )

    def downward(g):
        return pltpu.make_async_remote_copy(
            src_ref=zout.at[g], dst_ref=zin.at[g], send_sem=zs.at[g], recv_sem=zr.at[g],
            device_id={"lev": lax.rem(lev + 1, depth)}, device_id_type=pl.DeviceIdType.MESH,
        )

    def own_out(c):
        return pltpu.make_async_copy(outb.at[core, local(c)], out_ref.at[part(c, core)], own2.at[c])

    def swap_out(c):
        return pltpu.make_async_remote_copy(
            src_ref=outb.at[1 - core, local(c)], dst_ref=out_ref.at[part(c, core)],
            send_sem=hs.at[c], recv_sem=hr.at[c],
            device_id={"lon": partner}, device_id_type=pl.DeviceIdType.MESH,
        )

    scalars = [
        pltpu.make_async_copy(source, held, small.at[i])
        for i, (source, held) in enumerate((
            (table_hbm, table_ref), (fraction_hbm, fraction_ref),
            (class_hbm, class_ref), (thick_hbm, thick_ref)))
    ]
    barrier = pltpu.get_barrier_semaphore()
    pl.semaphore_signal(barrier, inc=1, device_id={"lon": partner}, device_id_type=pl.DeviceIdType.MESH)
    for d in range(1, chips):
        pl.semaphore_signal(barrier, inc=1, device_id={"lon": peer(d)}, device_id_type=pl.DeviceIdType.MESH)
    for k in (1, depth - 1):
        pl.semaphore_signal(barrier, inc=1, device_id={"lev": lax.rem(lev + k, depth)},
                            device_id_type=pl.DeviceIdType.MESH)
    head_in = pltpu.make_async_copy(head_ref, xin.at[:, local(0)], own1.at[0])
    head_in.start()
    for copy in scalars:
        copy.start()
    for c in range(1, chunks):
        own_in(c).start()

    def ratios(tracer):
        bin_class = jnp.full((SUB, width), class_ref[tracer // GROUPS], jnp.int32)
        speed = 0.5
        for b in range(3):
            speed = speed * jnp.where((bin_class & (1 << b)) != 0, 2.0 ** (1 << b), 1.0)
        return [speed / thick_ref[level] for level in range(levels)]

    def rolls(value, by):
        return pltpu.roll(value, by, axis=1)

    def spread(c):
        first, size = parts[c]

        @pl.loop(0, lats, unroll=8 // size)
        def _(j):
            for side in (0, 1):
                for g in range(size):
                    value = xin[side, first + g, pl.ds(j, SUB, stride=lats), :]
                    at = pl.ds(g * SUB, SUB)
                    xe[2 * j + side, at] = value
                    pools[c][2 * j + side, at] = value

    def pack(c):
        size = parts[c][1]
        lane = lax.broadcasted_iota(jnp.int32, (size * SUB, width), 1)
        unroll = 8 // size
        rounded = -(-slots // unroll) * unroll

        @pl.loop(1, chips)
        def _(d):
            @pl.loop(0, rounded, unroll=unroll)
            def _(i):
                e = (d - 1) * slots + i
                value = None
                for k in reversed(range(SEGMENTS)):
                    word = table_ref[3 + k * entry_rows + lax.div(e, width), lax.rem(e, width)]
                    piece = rolls(xe[word & (own - 1), pl.ds(0, size * SUB)], (word >> 7) & (width - 1))
                    value = piece if value is None else jnp.where(lane < (word >> 14), piece, value)
                sends[c][e] = value

            onward(c, d).start()

    def unpack(c):
        first, size = parts[c]
        pool = pools[c]
        lane = lax.broadcasted_iota(jnp.int32, (size * SUB, width), 1)
        edge = lane == 0

        def piece(word):
            at = word & 511
            both = jnp.where(lane >= ((word >> 9) & (width - 1)), pool[at], pool[at + 1])
            return rolls(both, word >> 16)

        @pl.loop(0, lats, unroll=16 // size)
        def _(j):
            share = fraction_ref[j]
            rest = table_ref[2, j]
            full = rolls(pool[table_ref[0, j]], rest)
            high = piece(table_ref[1, j])
            low = piece(table_ref[1, lats + j])
            left = jnp.where(lane < rest, low, full)
            right = jnp.where(lane < rest, full, high)
            left_turned = rolls(left, 1)
            left_before = jnp.where(edge, rolls(low, 1), left_turned)
            right_before = jnp.where(edge, left_turned, rolls(right, 1))
            left = (1.0 - share) * left + share * left_before
            right = (1.0 - share) * right + share * right_before
            for g in range(size):
                outb[0, first + g, pl.ds(j, SUB, stride=lats), :] = left[g * SUB:(g + 1) * SUB]
                outb[1, first + g, pl.ds(j, SUB, stride=lats), :] = right[g * SUB:(g + 1) * SUB]

    def rows(tt, level, i):
        return pl.ds(pl.multiple_of((tt * levels + level) * lats + i * SUB, SUB), SUB)

    def bottom(side, tt, i):
        return pl.ds(pl.multiple_of((side * each + tt) * lats + i * SUB, SUB), SUB)

    def settle(held, c):
        @pl.loop(parts[c][0], sum(parts[c]))
        def _(g):
            for tt in range(each):
                ratio = ratios((core * groups + g) * each + tt)
                keep = [1.0 / (1.0 + r) for r in ratio]
                carry = [r * k for r, k in zip(ratio, keep)]

                @pl.loop(0, lats // SUB, unroll=2)
                def _(i):
                    for side in (0, 1):
                        value = None
                        for level in range(levels):
                            field = keep[level] * held[side, g, rows(tt, level, i), :]
                            value = field if value is None else field + carry[level] * value
                            held[side, g, rows(tt, level, i), :] = value
                        zout[g, bottom(side, tt, i), :] = value

            @pl.when((lev == 0) & (depth > 1))
            def _():
                downward(g).start()

    def sink(held, c):
        def reach_of(g, tt):
            reach = []
            for r in ratios((core * groups + g) * each + tt):
                step = r / (1.0 + r)
                reach.append(reach[-1] * step if reach else step)
            return reach

        @pl.when(lev > 0)
        def _():
            @pl.loop(parts[c][0], sum(parts[c]))
            def _(g):
                downward(g).wait_recv()
                for tt in range(each):
                    last = reach_of(g, tt)[-1]

                    @pl.loop(0, lats // SUB, unroll=2)
                    def _(i):
                        for side in (0, 1):
                            at = bottom(side, tt, i)
                            value = zout[g, at, :] + last * zin[g, at, :]
                            zout[g, at, :] = value
                            held[side, g, rows(tt, levels - 1, i), :] = value

                @pl.when(lev < depth - 1)
                def _():
                    downward(g).start()

        @pl.when(lev > 0)
        def _():
            @pl.loop(parts[c][0], sum(parts[c]))
            def _(g):
                for tt in range(each):
                    reach = reach_of(g, tt)

                    @pl.loop(0, lats // SUB, unroll=2)
                    def _(i):
                        for side in (0, 1):
                            above = zin[g, bottom(side, tt, i), :]
                            for level in range(levels - 1):
                                held[side, g, rows(tt, level, i), :] += reach[level] * above

    def arrive(c):
        if c == 0:
            head_in.wait()
            return
        own_in(c).wait()
        swap_in(c).wait_recv()

    for c in range(late):
        arrive(c)
        spread(c)
        if c == 0:
            for copy in scalars:
                copy.wait()
            pl.semaphore_wait(barrier, chips + 2)
            for later in range(1, chunks):
                swap_in(later).start()
        pack(c)
        if c == 0:
            for later in range(late, chunks):
                arrive(later)
                settle(xin, later)
    for c in range(late, chunks):
        sink(xin, c)
        spread(c)
        pack(c)
    for c in range(chunks):
        @pl.loop(1, chips)
        def _(d):
            onward(c, d).wait_recv()

        unpack(c)
        if c < late:
            settle(outb, c)
            sink(outb, c)
        own_out(c).start()
        swap_out(c).start()

    @pl.when(lev < depth - 1)
    def _():
        @pl.loop(0, groups)
        def _(g):
            downward(g).wait_send()

    for c in range(chunks):
        if c:
            swap_in(c).wait_send()

        @pl.loop(1, chips)
        def _(d):
            onward(c, d).wait_send()

        own_out(c).wait()
        swap_out(c).wait()


def in_hbm(arrays):
    return tuple(pltpu.with_memory_space_constraint(a, pltpu.HBM) for a in arrays)


def make_plan(offsets, blocks, chips, tiers):
    lats = offsets.shape[0]
    count, span, width = blocks.shape
    words = -(-(chips - 1) * tiers[-1] // width)
    return pl.pallas_call(
        functools.partial(plan_kernel, chips, tiers, lats, count // 2),
        out_shape=(
            jax.ShapeDtypeStruct((3 + SEGMENTS * words, width), jnp.int32),
            jax.ShapeDtypeStruct((1,), jnp.int32),
            jax.ShapeDtypeStruct((2, 1, span, width), jnp.float32),
        ),
        in_specs=[pl.BlockSpec(memory_space=pltpu.SMEM), pl.BlockSpec(memory_space=pltpu.HBM)],
        out_specs=(
            pl.BlockSpec(memory_space=pltpu.VMEM),
            pl.BlockSpec(memory_space=pltpu.SMEM),
            pl.BlockSpec(memory_space=pl.ANY),
        ),
        scratch_shapes=[pltpu.VMEM((2 * lats, width), jnp.int32)] + [pltpu.SemaphoreType.DMA] * 3,
        compiler_params=pltpu.CompilerParams(collective_id=len(tiers) + 1, has_side_effects=True),
    )(offsets, *in_hbm((blocks,)))


def direct(slots, identity, tracers, head, table, fraction, bin_class, thickness):
    count, levels, lats, width = tracers.shape
    n = lax.axis_size("lon")
    depth = lax.axis_size("lev")
    chips = n // 2
    groups = count * levels // (2 * SUB)
    chunks = chunks_of(groups)
    span = SUB * lats
    entries = (chips - 1) * slots
    hbm = pl.BlockSpec(memory_space=pltpu.HBM)
    held = [pltpu.SMEM(a.shape, a.dtype) for a in (table, fraction, bin_class, thickness)]
    sem = pltpu.SemaphoreType.DMA
    many = sem((len(chunks),))
    edge = 2 * (SUB // levels) * lats

    def vmem(*shape):
        return pltpu.VMEM((*shape, width), jnp.float32)

    out = pl.pallas_call(
        functools.partial(direct_kernel, n, depth, slots, lats, levels),
        out_shape=jax.ShapeDtypeStruct((2 * groups, span, width), jnp.float32),
        in_specs=[hbm, pl.BlockSpec(memory_space=pl.ANY), *[hbm] * 4],
        out_specs=pl.BlockSpec(memory_space=pl.ANY),
        scratch_shapes=[
            *held, sem((4,)),
            vmem(2, groups, span), vmem(2 * lats, 2 * SUB), vmem(2, groups, span),
            vmem(groups, edge), vmem(groups, edge),
            many, many, many, sem((len(chunks), chips)), sem((len(chunks), chips)),
            sem((groups,)), sem((groups,)), many, many, many,
            *[vmem(entries + 8, size * SUB) for _, size in chunks],
            *[vmem(2 * lats + entries + 1, size * SUB) for _, size in chunks],
        ],
        compiler_params=pltpu.CompilerParams(
            collective_id=identity, has_side_effects=True, vmem_limit_bytes=44 << 20),
    )(*in_hbm((tracers.reshape(2 * groups, span, width),)), head, *in_hbm((table, fraction, bin_class, thickness)))
    return out.reshape(tracers.shape)


def on_device(tracers, offsets, fraction, bin_class, thickness):
    count, levels, lats, width = tracers.shape
    n = lax.axis_size("lon")
    if width != 128 or lats != 64 or n % 2 or n < 4 or SUB % levels or count * levels % (2 * SUB):
        return by_tracer(tracers, offsets, fraction, bin_class, thickness)
    tiers = []
    for share in SHARES:
        slots = -(-share * lats // (16 * (n // 2)))
        slots += slots % 2
        if slots not in tiers:
            tiers.append(slots)
    blocks = tracers.reshape(count * levels // SUB, SUB * lats, width)
    table, tier, head = make_plan(offsets, blocks, n // 2, tiers)
    ways = [
        functools.partial(lambda slots, i, x, o, a, t, f, b, h: direct(slots, i, x, a, t, f, b, h), slots, i + 1)
        for i, slots in enumerate(tiers)
    ]
    ways.append(lambda x, o, a, t, f, b, h: by_tracer(x, o, f, b, h))
    return lax.switch(tier[0], ways, tracers, offsets, head, table, fraction, bin_class, thickness)


def solution(mesh):
    in_specs = (P(None, "lev", None, "lon"), P(), P(), P(), P("lev"))
    out_specs = P(None, "lev", None, "lon")
    return jax.shard_map(
        on_device, mesh=mesh, in_specs=in_specs, out_specs=out_specs, check_vma=False
    )
```
